32 devices in a mesh: proc: 8 (over z, y), loss: 2 (over x), vars: 2 (over core).
Axes of the slice: x: 2, y: 2, z: 4, core: 2. Of those that a mesh axis runs over, the one named last changes fastest.
Arguments:
- tokens: bfloat16 [16, 360, 1536], P('proc'), may hold values from -6 to 6
- shift: int32 [1], replicated, may hold values from 0 to 11
- w_qkv: bfloat16 [1536, 3, 16, 96], P(None, None, ('loss', 'vars')), may hold values from -0.15625 to 0.15625
- w_proj: bfloat16 [16, 96, 1536], replicated, may hold values from -0.15625 to 0.15625
- ln_gain: float32 [1536], replicated, may hold values from 0.1 to 1.9
- w_dec: bfloat16 [64, 4, 4, 1536], P(('loss', 'vars')), may hold values from -0.15625 to 0.15625
- prediction: bfloat16 [64, 64, 1440], P(('loss', 'vars'), 'proc'), may hold values from -6 to 6
- target: float32 [64, 64, 1440], P(('loss', 'vars'), 'proc'), may hold values from -12 to 12
- legendre: float32 [128, 64, 384], P('proc'), may hold values from -0.75 to 0.75
Outputs:
- amse: float32 [64], P(('loss', 'vars'))
- field_grad: float32 [64, 64, 1440], P(('loss', 'vars'), 'proc')
- input_grad: bfloat16 [16, 360, 1536], P('proc', None, ('loss', 'vars'))
The draws below stay inside these ranges and needn't reach their ends.
Inputs may be any that keep to these rules, and one draw needn't show every extreme that they name: `shift`: the offset is the same for all tokens.
All inputs are finite; a program needn't handle non-finite values.
Results may differ from the reference program's by a relative error of at most 0.012.
Values may be sent and summed in bfloat16 or wider, within the bound.
A program may use at most 128 MiB of HBM per device.

```python
import math
import jax
import jax.numpy as jnp
from jax import lax

D = 1536
HEADS = 16
HEAD = 96
VARS = 64
LON = 1440
LDEG = 384
WR = 2
WC = 12
TC = 360
TR = 16
LAT = 64
MODES = 128


def shard_levels(own_key, dims, shards, least, largest):
    factor_of, own = 1.0, jax.random.fold_in(own_key, 6)
    for axis_at, blocks in shards:
        steps = jnp.exp(jax.random.uniform(jax.random.fold_in(own, axis_at), (blocks,), jnp.float32, least / len(shards), largest / len(shards)))
        factor_of = factor_of * jnp.repeat(steps, dims[axis_at] // blocks).reshape([-1 if axis == axis_at else 1 for axis in range(len(dims))])
    return factor_of


def gaussian(stream_key, shape, width, reach, shards=(), kind=jnp.bfloat16):
    drawn = jax.random.normal(stream_key, shape, jnp.float32) * width
    if len(shards) > 0:
        drawn = shard_levels(stream_key, shape, shards, -0.22, 0.18) * drawn
    return jnp.clip(drawn, min=-reach, max=reach).astype(kind)


def setup_inputs(seed: int = 0) -> dict:
    key_list = jax.random.split(jax.random.key(seed), 10)
    return {
        "tokens": gaussian(key_list[0], (TR, TC, D), 1.0, 6.0, ((0, 8),)),
        "shift": jax.random.randint(key_list[1], (1,), 0, WC).astype(jnp.int32),
        "w_qkv": gaussian(key_list[2], (D, 3, HEADS, HEAD), D ** -0.5, 0.15625, ((2, 4),)),
        "w_proj": gaussian(key_list[3], (HEADS, HEAD, D), D ** -0.5, 0.15625),
        "ln_gain": jnp.clip(1.0 + 0.18 * jax.random.normal(key_list[4], (D,), jnp.float32), 0.1, 1.9),
        "w_dec": gaussian(key_list[5], (VARS, 4, 4, D), D ** -0.5, 0.15625, ((0, 4),)),
        "prediction": gaussian(key_list[6], (VARS, LAT, LON), 1.0, 6.0, ((0, 4), (1, 8))),
        "target": gaussian(key_list[7], (VARS, LAT, LON), 2.0, 12.0, ((0, 4), (1, 8)), jnp.float32),
        "legendre": gaussian(key_list[8], (MODES, LAT, LDEG), LAT ** -0.5, 0.75, ((0, 8),), jnp.float32),
    }


EPSILON = 1e-06
NORM_EPSILON = 1e-05
HIGHEST = lax.Precision.HIGHEST

def fourier_basis(mode_count):
    column = jnp.arange(LON, dtype=jnp.int32)
    wavenumber = jnp.arange(mode_count, dtype=jnp.int32)
    phase = (column[:, None] * wavenumber[None, :] % LON).astype(jnp.float32) * (2.0 * math.pi / LON)
    norm_factor = 1.0 / math.sqrt(LON)
    return jnp.stack([jnp.cos(phase) * norm_factor, -jnp.sin(phase) * norm_factor])

def amse_terms(power_pred, power_true, crossed):
    amp_pred = jnp.sqrt(power_pred + EPSILON)
    amp_true = jnp.sqrt(power_true + EPSILON)
    return (amp_pred - amp_true) ** 2 + 2.0 * jnp.maximum(power_pred, power_true) * (1.0 - crossed / (amp_pred * amp_true))

def spectral_loss(field_values, target, legendre, fourier):
    fields = jnp.stack([field_values, target])
    spectra = jnp.einsum('fvao,com->fvacm', fields, fourier, precision=HIGHEST)
    harmonics = jnp.einsum('fvacm,mal->fvmcl', spectra, legendre, precision=HIGHEST)
    power_pred = lax.optimization_barrier(jnp.sum(harmonics[0] ** 2, axis=(1, 2)))
    power_true = lax.optimization_barrier(jnp.sum(harmonics[1] ** 2, axis=(1, 2)))
    crossed = lax.optimization_barrier(jnp.sum(harmonics[0] * harmonics[1], axis=(1, 2)))
    per_var = lax.optimization_barrier(jnp.sum(amse_terms(power_pred, power_true, crossed), axis=-1)) / (LDEG * MODES)
    return (jnp.mean(per_var), per_var)

def norm_parts(rolled, ln_gain):
    values = rolled.astype(jnp.float32)
    centre = lax.optimization_barrier(jnp.mean(values, axis=-1, keepdims=True))
    centred = values - centre
    variance = lax.optimization_barrier(jnp.mean(centred * centred, axis=-1, keepdims=True))
    inv_std = lax.rsqrt(variance + NORM_EPSILON)
    normed = centred * inv_std
    return (normed, inv_std, (normed * ln_gain).astype(jnp.bfloat16))

def norm_backward(grad_normed, normed, inv_std, ln_gain):
    scaled = grad_normed * ln_gain
    return inv_std * (scaled - lax.optimization_barrier(jnp.mean(scaled, axis=-1, keepdims=True)) - normed * lax.optimization_barrier(jnp.mean(scaled * normed, axis=-1, keepdims=True)))

def to_windows(values):
    row_count, col_count = (values.shape[0], values.shape[1])
    trailing = values.shape[2:]
    shaped = values.reshape((row_count // WR, WR, col_count // WC, WC) + trailing)
    shaped = jnp.moveaxis(shaped, 2, 1)
    return shaped.reshape((row_count // WR * (col_count // WC), WR * WC) + trailing)

def from_windows(values, row_count, col_count):
    trailing = values.shape[2:]
    shaped = values.reshape((row_count // WR, col_count // WC, WR, WC) + trailing)
    shaped = jnp.moveaxis(shaped, 1, 2)
    return shaped.reshape((row_count, col_count) + trailing)

def window_backward(queries, key_win, value_win, grad_out):
    score_scale = HEAD ** (-0.5)
    scores = jnp.einsum('nihe,njhe->nhij', queries.astype(jnp.float32), key_win.astype(jnp.float32)) * score_scale
    weights = jnp.exp(scores)
    weights = weights / lax.optimization_barrier(jnp.sum(weights, axis=-1, keepdims=True))
    rounded = weights.astype(jnp.bfloat16)
    grad_values = jnp.einsum('nhij,nihe->njhe', rounded.astype(jnp.float32), grad_out.astype(jnp.float32)).astype(jnp.bfloat16)
    grad_weights = jnp.einsum('nihe,njhe->nhij', grad_out.astype(jnp.float32), value_win.astype(jnp.float32))
    grad_scores = weights * (grad_weights - lax.optimization_barrier(jnp.sum(weights * grad_weights, axis=-1, keepdims=True)))
    score_round = (grad_scores * score_scale).astype(jnp.bfloat16)
    grad_queries = jnp.einsum('nhij,njhe->nihe', score_round.astype(jnp.float32), key_win.astype(jnp.float32)).astype(jnp.bfloat16)
    grad_keys = jnp.einsum('nhij,nihe->njhe', score_round.astype(jnp.float32), queries.astype(jnp.float32)).astype(jnp.bfloat16)
    return (grad_queries, grad_keys, grad_values)

def reference(tokens, shift, w_qkv, w_proj, ln_gain, w_dec, prediction, target, legendre):
    fourier = fourier_basis(MODES)
    pred_field = prediction.astype(jnp.float32)

    def total_loss(field_values):
        return spectral_loss(field_values, target, legendre, fourier)[0]
    amse = spectral_loss(pred_field, target, legendre, fourier)[1]
    field_grad = jax.grad(total_loss)(pred_field) * (LAT * LON)
    grad_round = field_grad.astype(jnp.bfloat16)
    row_count, col_count = (tokens.shape[0], tokens.shape[1])
    grad_tiles = grad_round.reshape(VARS, row_count, 4, col_count, 4)
    token_grad = jnp.einsum('vrato,vaod->rtd', grad_tiles.astype(jnp.float32), w_dec.astype(jnp.float32))
    offset = shift[0]
    rolled_grad = jnp.roll(token_grad, -offset, axis=1)
    normed, inv_std, norm_out = norm_parts(jnp.roll(tokens, -offset, axis=1), ln_gain)
    projected = jnp.einsum('rtd,dkhe->rtkhe', norm_out.astype(jnp.float32), w_qkv.astype(jnp.float32)).astype(jnp.bfloat16)
    grad_out = jnp.einsum('rtd,hed->rthe', rolled_grad, w_proj.astype(jnp.float32), precision=HIGHEST).astype(jnp.bfloat16)
    grad_queries, grad_keys, grad_values = window_backward(to_windows(projected[:, :, 0]), to_windows(projected[:, :, 1]), to_windows(projected[:, :, 2]), to_windows(grad_out))
    stacked = jnp.stack([from_windows(grad_queries, row_count, col_count), from_windows(grad_keys, row_count, col_count), from_windows(grad_values, row_count, col_count)], axis=2)
    grad_normed = jnp.einsum('rtkhe,dkhe->rtd', stacked.astype(jnp.float32), w_qkv.astype(jnp.float32))
    summed = rolled_grad + norm_backward(grad_normed, normed, inv_std, ln_gain)
    input_grad = jnp.roll(summed, offset, axis=1).astype(jnp.bfloat16)
    return (amse, field_grad, input_grad)
```

```python
import functools
import math

import jax
import jax.numpy as jnp
import numpy as np
from jax import lax
from jax.experimental import pallas as pl
from jax.experimental.pallas import tpu as pltpu
from jax.sharding import PartitionSpec as P

HEAD = 96
VARS = 64
LON = 1440
LDEG = 384
WR = 2
WC = 12

EPSILON = 1e-06
NORM_EPSILON = 1e-05
HIGHEST = lax.Precision.HIGHEST
MESH = pl.DeviceIdType.MESH
F32 = jnp.float32
BF16 = jnp.bfloat16
VMEM = pl.BlockSpec(memory_space=pltpu.VMEM)
NT = (((1,), (1,)), ((), ()))


def fourier_basis(mode_count):
    column = np.arange(LON, dtype=np.int64)
    wavenumber = np.arange(mode_count, dtype=np.int64)
    phase = (column[:, None] * wavenumber[None, :] % LON) * (2.0 * math.pi / LON)
    return np.stack([np.cos(phase), -np.sin(phase)]) / math.sqrt(LON)


def amse_terms(power_pred, power_true, crossed):
    amp_pred = jnp.sqrt(power_pred + EPSILON)
    amp_true = jnp.sqrt(power_true + EPSILON)
    return (amp_pred - amp_true) ** 2 + 2.0 * jnp.maximum(power_pred, power_true) * (
        1.0 - crossed / (amp_pred * amp_true)
    )


def place(axis, index, sizes):
    proc, loss, var = (lax.axis_index(name) for name in ("proc", "loss", "vars"))
    if axis == "proc":
        return (index, loss, var)
    if axis == "loss":
        return (proc, index, var)
    if axis == "vars":
        return (proc, loss, index)
    return (proc, index // sizes["vars"], lax.rem(index, sizes["vars"]))


def rank(axis, sizes):
    if axis == "group":
        return lax.axis_index("loss") * sizes["vars"] + lax.axis_index("vars")
    return lax.axis_index(axis)


def greet(pairs):
    barrier = pltpu.get_barrier_semaphore()
    for device in pairs:
        pl.semaphore_signal(barrier, inc=1, device_id=device, device_id_type=MESH)
    pl.semaphore_wait(barrier, len(pairs))


def exchange_kernel(axis, count, sizes, spread, x_ref, out_ref, send, recv, own):
    me = rank(axis, sizes)
    peers = [lax.rem(me + k, count) for k in range(1, count)]
    greet([place(axis, peer, sizes) for peer in peers])
    copies = []
    for k, peer in enumerate(peers):
        copies.append(
            pltpu.make_async_remote_copy(
                src_ref=x_ref if spread else x_ref.at[peer],
                dst_ref=out_ref.at[me],
                send_sem=send.at[k],
                recv_sem=recv.at[k],
                device_id=place(axis, peer, sizes),
                device_id_type=MESH,
            )
        )
        copies[-1].start()
    local = pltpu.make_async_copy(x_ref if spread else x_ref.at[me], out_ref.at[me], own)
    local.start()
    local.wait()
    for copy in copies:
        copy.wait()


def exchange(x, axis, sizes, collective_id, spread=False):
    count = sizes["loss"] * sizes["vars"] if axis == "group" else sizes[axis]
    shape = (count,) + x.shape if spread else x.shape
    return pl.pallas_call(
        functools.partial(exchange_kernel, axis, count, sizes, spread),
        out_shape=jax.ShapeDtypeStruct(shape, x.dtype),
        in_specs=[VMEM],
        out_specs=VMEM,
        scratch_shapes=[
            pltpu.SemaphoreType.DMA((count - 1,)),
            pltpu.SemaphoreType.DMA((count - 1,)),
            pltpu.SemaphoreType.DMA,
        ],
        compiler_params=pltpu.CompilerParams(
            collective_id=collective_id, has_side_effects=True
        ),
        name="exchange_%d" % collective_id,
    )(x)


def total_kernel(count, sizes, x_ref, out_ref, parts, acc, send, recv, send2, recv2, own):
    me = rank("proc", sizes)
    peers = [lax.rem(me + k, count) for k in range(1, count)]
    greet([place("proc", peer, sizes) for peer in peers])

    def copy(src, dst, sems, k, peer):
        made = pltpu.make_async_remote_copy(
            src_ref=src,
            dst_ref=dst,
            send_sem=sems[0].at[k],
            recv_sem=sems[1].at[k],
            device_id=place("proc", peer, sizes),
            device_id_type=MESH,
        )
        made.start()
        return made

    first = [copy(x_ref.at[peer], parts.at[k], (send, recv), k, peer) for k, peer in enumerate(peers)]
    for made in first:
        made.wait()
    value = x_ref[me]
    for k in range(count - 1):
        value = value + parts[k]
    acc[...] = value
    second = [copy(acc, out_ref.at[me], (send2, recv2), k, peer) for k, peer in enumerate(peers)]
    local = pltpu.make_async_copy(acc, out_ref.at[me], own)
    local.start()
    local.wait()
    for made in second:
        made.wait()


def proc_total(x, sizes, collective_id):
    count = sizes["proc"]
    sems = [pltpu.SemaphoreType.DMA((count - 1,)) for _ in range(4)]
    return pl.pallas_call(
        functools.partial(total_kernel, count, sizes),
        out_shape=jax.ShapeDtypeStruct(x.shape, x.dtype),
        in_specs=[VMEM],
        out_specs=VMEM,
        scratch_shapes=[
            pltpu.VMEM((count - 1,) + x.shape[1:], x.dtype),
            pltpu.VMEM(x.shape[1:], x.dtype),
        ]
        + sems
        + [pltpu.SemaphoreType.DMA],
        compiler_params=pltpu.CompilerParams(
            collective_id=collective_id, has_side_effects=True
        ),
        name="proc_total",
    )(x)


def scatter_kernel(blocks, sizes, p_ref, kept_ref, out_ref, got, mid, far, s1, r1, s2, r2):
    loss_count, var_count = sizes["loss"], sizes["vars"]
    loss, var = lax.axis_index("loss"), lax.axis_index("vars")
    near = [lax.rem(var + k, var_count) for k in range(1, var_count)]
    away = [lax.rem(loss + k, loss_count) for k in range(1, loss_count)]
    greet(
        [place("vars", peer, sizes) for peer in near]
        + [place("loss", peer, sizes) for peer in away]
    )
    first, second = [], []
    for b in range(blocks):
        row = []
        for k, peer in enumerate(near):
            row.append(
                pltpu.make_async_remote_copy(
                    src_ref=p_ref.at[b, peer],
                    dst_ref=got.at[b, k],
                    send_sem=s1.at[b, k],
                    recv_sem=r1.at[b, k],
                    device_id=place("vars", peer, sizes),
                    device_id_type=MESH,
                )
            )
            row[-1].start()
        first.append(row)
    for b in range(blocks):
        for made in first[b]:
            made.wait()
        for j in range(loss_count):
            value = p_ref[b, var, j].astype(F32)
            for k in range(var_count - 1):
                value = value + got[b, k, j].astype(F32)
            mid[b, j] = value.astype(BF16)
        row = []
        for k, peer in enumerate(away):
            row.append(
                pltpu.make_async_remote_copy(
                    src_ref=mid.at[b, peer],
                    dst_ref=far.at[b, k],
                    send_sem=s2.at[b, k],
                    recv_sem=r2.at[b, k],
                    device_id=place("loss", peer, sizes),
                    device_id_type=MESH,
                )
            )
            row[-1].start()
        second.append(row)
    for b in range(blocks):
        value = kept_ref[b] + mid[b, loss].astype(F32)
        for made in second[b]:
            made.wait()
        for k in range(loss_count - 1):
            value = value + far[b, k].astype(F32)
        out_ref[b] = value.astype(BF16)


def reduce_group(parts, kept, sizes, collective_id):
    blocks, var_count, loss_count, rows, width = parts.shape
    return pl.pallas_call(
        functools.partial(scatter_kernel, blocks, sizes),
        out_shape=jax.ShapeDtypeStruct(kept.shape, BF16),
        in_specs=[VMEM, VMEM],
        out_specs=VMEM,
        scratch_shapes=[
            pltpu.VMEM((blocks, var_count - 1, loss_count, rows, width), BF16),
            pltpu.VMEM((blocks, loss_count, rows, width), BF16),
            pltpu.VMEM((blocks, loss_count - 1, rows, width), BF16),
            pltpu.SemaphoreType.DMA((blocks, var_count - 1)),
            pltpu.SemaphoreType.DMA((blocks, var_count - 1)),
            pltpu.SemaphoreType.DMA((blocks, loss_count - 1)),
            pltpu.SemaphoreType.DMA((blocks, loss_count - 1)),
        ],
        compiler_params=pltpu.CompilerParams(
            collective_id=collective_id, has_side_effects=True
        ),
        name="reduce_group",
    )(parts, kept)


def harmonics_kernel(modes, var_count, spectra_ref, legendre_ref, harm_ref, power_ref):
    half = 2 * var_count
    sums = [jnp.zeros((half, LDEG), F32) for _ in range(3)]
    for m in range(modes):
        harm = jnp.dot(
            spectra_ref[m], legendre_ref[m], precision=HIGHEST, preferred_element_type=F32
        )
        harm_ref[m] = harm
        pred, true = harm[:half], harm[half:]
        sums = [sums[0] + pred * pred, sums[1] + true * true, sums[2] + pred * true]
    for i in range(3):
        power_ref[i] = sums[i][:var_count] + sums[i][var_count:]


def harmonics(spectra, legendre):
    modes, rows, _ = spectra.shape
    var_count = rows // 4
    return pl.pallas_call(
        functools.partial(harmonics_kernel, modes, var_count),
        out_shape=(
            jax.ShapeDtypeStruct((modes, rows, LDEG), F32),
            jax.ShapeDtypeStruct((3, var_count, LDEG), F32),
        ),
        in_specs=[VMEM, VMEM],
        out_specs=(VMEM, VMEM),
        name="harmonics",
    )(spectra, legendre)


def spectra_grad_kernel(modes, pack, procs, var_count, harm_ref, legendre_ref, gp_ref, gc_ref, out_ref):
    half = 2 * var_count
    gp = jnp.concatenate([gp_ref[...], gp_ref[...]], axis=0) * 2.0
    gc = jnp.concatenate([gc_ref[...], gc_ref[...]], axis=0)
    for hi in range(modes // pack):
        columns = []
        for lo in range(pack):
            m = hi * pack + lo
            harm = harm_ref[m]
            grad = gp * harm[:half] + gc * harm[half:]
            columns.append(
                lax.dot_general(
                    legendre_ref[m], grad, NT, precision=HIGHEST, preferred_element_type=F32
                )
            )
        block = jnp.concatenate(columns, axis=1)
        out_ref[:, hi] = block.reshape(procs, block.shape[0] // procs, block.shape[1])


def spectra_grad(harm, legendre, gp, gc, procs):
    modes, rows, _ = harm.shape
    lats = legendre.shape[1]
    var_count = rows // 4
    pack = min(modes, max(1, 128 // (2 * var_count)))
    return pl.pallas_call(
        functools.partial(spectra_grad_kernel, modes, pack, procs, var_count),
        out_shape=jax.ShapeDtypeStruct(
            (procs, modes // pack, lats // procs, pack * 2 * var_count), F32
        ),
        in_specs=[VMEM] * 4,
        out_specs=VMEM,
        name="spectra_grad",
    )(harm, legendre, gp, gc), pack


def attention_kernel(
    heads, cols, groups, f_ref, coeff_ref, mix_ref, proj_ref, tok_ref, gain_ref, w_ref, part_ref, kept_ref
):
    loss_count, var_count = groups
    rows = WR * cols
    pieces = []
    for o in range(4):
        y = jnp.dot(f_ref[o], coeff_ref[0], preferred_element_type=F32)
        half = y.shape[1] // WR
        pieces.append(
            jnp.concatenate([y[:, r * half : (r + 1) * half] for r in range(WR)], axis=0).astype(BF16)
        )
    tiles = jnp.concatenate(pieces, axis=1)
    mixed = jnp.dot(tiles, mix_ref[...], preferred_element_type=F32)
    width = heads * HEAD
    grad_out = mixed[:, :width].astype(BF16)
    kept_ref[0] = mixed[:, width:]

    window_i = lax.rem(lax.broadcasted_iota(jnp.int32, (rows, rows), 0), cols) // WC
    window_j = lax.rem(lax.broadcasted_iota(jnp.int32, (rows, rows), 1), cols) // WC
    same = window_i == window_j
    scale = HEAD ** (-0.5)
    grads = [[], [], []]
    for h in range(heads):
        q, k, v = (
            proj_ref[0, :, (i * heads + h) * HEAD : (i * heads + h + 1) * HEAD] for i in range(3)
        )
        go = grad_out[:, h * HEAD : (h + 1) * HEAD]
        scores = lax.dot_general(q, k, NT, preferred_element_type=F32) * scale
        weights = jnp.where(same, jnp.exp(scores), 0.0)
        weights = weights / jnp.sum(weights, axis=-1, keepdims=True)
        rounded = weights.astype(BF16)
        first = (((0,), (0,)), ((), ()))
        grads[2].append(
            lax.dot_general(rounded, go, first, preferred_element_type=F32).astype(BF16)
        )
        grad_weights = lax.dot_general(go, v, NT, preferred_element_type=F32)
        inner = jnp.sum(weights * grad_weights, axis=-1, keepdims=True)
        score_round = (weights * (grad_weights - inner) * scale).astype(BF16)
        grads[0].append(jnp.dot(score_round, k, preferred_element_type=F32).astype(BF16))
        grads[1].append(
            lax.dot_general(score_round, q, first, preferred_element_type=F32).astype(BF16)
        )
    stacked = jnp.concatenate(grads[0] + grads[1] + grads[2], axis=1)
    grad_normed = lax.dot_general(stacked, w_ref[...], NT, preferred_element_type=F32)

    values = tok_ref[0].astype(F32)
    centred = values - jnp.mean(values, axis=-1, keepdims=True)
    inv_std = lax.rsqrt(jnp.mean(centred * centred, axis=-1, keepdims=True) + NORM_EPSILON)
    normed = centred * inv_std
    scaled = grad_normed * gain_ref[...]
    local = inv_std * (
        scaled
        - jnp.mean(scaled, axis=-1, keepdims=True)
        - normed * jnp.mean(scaled * normed, axis=-1, keepdims=True)
    )
    local = local.astype(BF16)
    share = local.shape[1] // (loss_count * var_count)
    for l in range(loss_count):
        for v in range(var_count):
            at = (l * var_count + v) * share
            part_ref[0, v, l] = local[:, at : at + share]


def attention_backward(f_rolled, coeff, mix, projected, tokens, gain, w_flat, groups):
    blocks, rows, model = tokens.shape
    pairs = coeff.shape[0]
    cols = rows // WR
    per_pair = blocks // pairs
    depth = f_rolled.shape[2]
    width = projected.shape[2] // 3
    heads = width // HEAD
    loss_count, var_count = groups
    share = model // (loss_count * var_count)

    def whole(shape):
        return pl.BlockSpec(shape, lambda b: (0,) * len(shape))

    def per_block(shape):
        return pl.BlockSpec((1,) + shape, lambda b: (b,) + (0,) * len(shape))

    return pl.pallas_call(
        functools.partial(attention_kernel, heads, cols, groups),
        grid=(blocks,),
        in_specs=[
            pl.BlockSpec((4, cols, depth), lambda b: (0, lax.rem(b, per_pair), 0)),
            pl.BlockSpec((1,) + coeff.shape[1:], lambda b: (b // per_pair, 0, 0)),
            whole(mix.shape),
            per_block((rows, 3 * width)),
            per_block((rows, model)),
            whole(gain.shape),
            whole(w_flat.shape),
        ],
        out_specs=(
            per_block((var_count, loss_count, rows, share)),
            per_block((rows, share)),
        ),
        out_shape=(
            jax.ShapeDtypeStruct((blocks, var_count, loss_count, rows, share), BF16),
            jax.ShapeDtypeStruct((blocks, rows, share), F32),
        ),
        name="attention_backward",
    )(f_rolled, coeff, mix, projected, tokens, gain, w_flat)


def body(tokens, shift, w_qkv, w_proj, ln_gain, w_dec, prediction, target, legendre):
    sizes = {name: lax.axis_size(name) for name in ("proc", "loss", "vars")}
    procs = sizes["proc"]
    groups = (sizes["loss"], sizes["vars"])
    group_count = groups[0] * groups[1]
    modes = legendre.shape[0]
    lat_all = legendre.shape[1]
    modes_all = modes * procs
    var_count, lats = prediction.shape[0], prediction.shape[1]
    basis = fourier_basis(modes_all)
    row_count, col_count, model = tokens.shape
    offset = shift[0]
    head_local = w_qkv.shape[2]
    width = head_local * HEAD
    share = model // group_count

    to_modes = jnp.asarray(
        basis.reshape(2, LON, procs, modes).transpose(2, 0, 3, 1).reshape(-1, LON), F32
    )
    fields = jnp.concatenate([prediction.astype(F32), target]).reshape(-1, LON)
    spectra = lax.dot_general(to_modes, fields, NT, precision=HIGHEST)
    at_owner = exchange(spectra.reshape(procs, 2 * modes, -1), "proc", sizes, 1)
    at_owner = at_owner.reshape(procs, 2, modes, 2, var_count, lats).transpose(2, 3, 1, 4, 0, 5)
    harm, power = harmonics(at_owner.reshape(modes, 4 * var_count, lat_all), legendre)
    if power.size % (procs * 128) == 0:
        shaped = power.reshape(procs, -1, 128)
        power = proc_total(shaped, sizes, 2).reshape(power.shape)
    else:
        power = lax.psum(power, "proc")
    degree_terms, pullback = jax.vjp(amse_terms, power[0], power[1], power[2])
    amse = jnp.sum(degree_terms, axis=-1) / (LDEG * modes_all)
    weight_grad = lat_all * LON / (VARS * LDEG * modes_all)
    grad_pred, _, grad_cross = pullback(jnp.full(degree_terms.shape, weight_grad, F32))
    grad_spectra, pack = spectra_grad(harm, legendre, grad_pred, grad_cross, procs)
    banded = exchange(grad_spectra, "proc", sizes, 3)
    banded = banded.reshape(procs, modes // pack, lats, pack, 2, var_count)
    banded = banded.transpose(0, 1, 3, 4, 5, 2).reshape(2 * modes_all, var_count, lats)

    pairs = row_count // WR
    sent = banded.astype(BF16).reshape(2 * modes_all, var_count, pairs, WR, 4)
    sent = sent.transpose(0, 2, 3, 1, 4).reshape(2 * modes_all, -1)
    coeff = exchange(sent, "group", sizes, 4, spread=True)
    coeff = coeff.reshape(group_count, 2 * modes_all, pairs, WR, 4 * var_count)
    coeff = coeff.transpose(2, 1, 3, 0, 4).reshape(pairs, 2 * modes_all, -1)

    by_mode = basis.transpose(1, 2, 0).reshape(LON, 2 * modes_all)
    field_grad = lax.dot_general(
        banded.reshape(2 * modes_all, -1),
        jnp.asarray(by_mode, F32),
        (((0,), (1,)), ((), ())),
        precision=HIGHEST,
    ).reshape(var_count, lats, LON)

    decoder = w_dec.transpose(2, 0, 1, 3).reshape(4 * var_count * 4, model)
    through = lax.dot_general(
        decoder, w_proj.reshape(-1, model), NT, preferred_element_type=F32
    ).astype(BF16)
    mix = jnp.concatenate(
        [
            through.reshape(-1, group_count, width),
            decoder.reshape(-1, group_count, share),
        ],
        axis=2,
    ).transpose(1, 0, 2)
    mix = exchange(mix, "group", sizes, 5)
    mix = mix.reshape(group_count, 4, 4 * var_count, width + share).transpose(1, 0, 2, 3)
    mix = mix.reshape(-1, width + share)

    cols = 120
    split = (pairs, WR, col_count // cols, cols)
    rolled = jnp.roll(tokens, -offset, axis=1)
    rolled = rolled.reshape(split + (model,)).transpose(0, 2, 1, 3, 4)
    rolled = rolled.reshape(-1, WR * cols, model)
    values = rolled.astype(F32)
    centred = values - jnp.mean(values, axis=-1, keepdims=True)
    inv_std = lax.rsqrt(jnp.mean(centred * centred, axis=-1, keepdims=True) + NORM_EPSILON)
    norm_out = (centred * inv_std * ln_gain).astype(BF16)
    w_flat = w_qkv.reshape(model, 3 * width)
    projected = jnp.einsum(
        "brd,dk->brk", norm_out, w_flat, preferred_element_type=F32
    ).astype(BF16)
    by_column = jnp.asarray(
        by_mode.reshape(col_count, 4, 2 * modes_all).transpose(1, 0, 2), BF16
    )
    f_rolled = jnp.roll(by_column, -offset, axis=1)
    parts, kept = attention_backward(
        f_rolled, coeff, mix, projected, rolled, ln_gain.reshape(1, model), w_flat, groups
    )
    summed = reduce_group(parts, kept, sizes, 6)
    summed = summed.reshape(pairs, col_count // cols, WR, cols, share).transpose(0, 2, 1, 3, 4)
    input_grad = jnp.roll(summed.reshape(row_count, col_count, share), offset, axis=1)
    return (amse, field_grad, input_grad)


def solution(mesh):
    return jax.shard_map(
        body,
        mesh=mesh,
        in_specs=(
            P("proc", None, None),
            P(),
            P(None, None, ("loss", "vars"), None),
            P(),
            P(),
            P(("loss", "vars"), None, None, None),
            P(("loss", "vars"), "proc", None),
            P(("loss", "vars"), "proc", None),
            P("proc", None, None),
        ),
        out_specs=(
            P(("loss", "vars")),
            P(("loss", "vars"), "proc", None),
            P("proc", None, ("loss", "vars")),
        ),
        check_vma=False,
    )
```

```python
import functools
import math

import jax
import jax.numpy as jnp
import numpy as np
from jax import lax
from jax.experimental import pallas as pl
from jax.experimental.pallas import tpu as pltpu
from jax.sharding import PartitionSpec as P

HEAD = 96
VARS = 64
LON = 1440
LDEG = 384
WR = 2
WC = 12

EPSILON = 1e-06
NORM_EPSILON = 1e-05
HIGHEST = lax.Precision.HIGHEST
MESH = pl.DeviceIdType.MESH
F32 = jnp.float32
BF16 = jnp.bfloat16
VMEM = pl.BlockSpec(memory_space=pltpu.VMEM)
NT = (((1,), (1,)), ((), ()))


def fourier_basis(mode_count):
    column = np.arange(LON, dtype=np.int64)
    wavenumber = np.arange(mode_count, dtype=np.int64)
    phase = (column[:, None] * wavenumber[None, :] % LON) * (2.0 * math.pi / LON)
    return np.stack([np.cos(phase), -np.sin(phase)]) / math.sqrt(LON)


def amse_terms(power_pred, power_true, crossed):
    amp_pred = jnp.sqrt(power_pred + EPSILON)
    amp_true = jnp.sqrt(power_true + EPSILON)
    return (amp_pred - amp_true) ** 2 + 2.0 * jnp.maximum(power_pred, power_true) * (
        1.0 - crossed / (amp_pred * amp_true)
    )


def place(axis, index, sizes):
    proc, loss, var = (lax.axis_index(name) for name in ("proc", "loss", "vars"))
    if axis == "proc":
        return (index, loss, var)
    if axis == "loss":
        return (proc, index, var)
    if axis == "vars":
        return (proc, loss, index)
    return (proc, index // sizes["vars"], lax.rem(index, sizes["vars"]))


def rank(axis, sizes):
    if axis == "group":
        return lax.axis_index("loss") * sizes["vars"] + lax.axis_index("vars")
    return lax.axis_index(axis)


def greet(pairs):
    barrier = pltpu.get_barrier_semaphore()
    for device in pairs:
        pl.semaphore_signal(barrier, inc=1, device_id=device, device_id_type=MESH)
    pl.semaphore_wait(barrier, len(pairs))


def exchange_kernel(axis, count, sizes, spread, x_ref, out_ref, send, recv, own):
    me = rank(axis, sizes)
    peers = [lax.rem(me + k, count) for k in range(1, count)]
    greet([place(axis, peer, sizes) for peer in peers])
    copies = []
    for k, peer in enumerate(peers):
        copies.append(
            pltpu.make_async_remote_copy(
                src_ref=x_ref if spread else x_ref.at[peer],
                dst_ref=out_ref.at[k + 1] if spread else out_ref.at[me],
                send_sem=send.at[k],
                recv_sem=recv.at[k],
                device_id=place(axis, peer, sizes),
                device_id_type=MESH,
            )
        )
        copies[-1].start()
    if spread:
        local = pltpu.make_async_copy(x_ref, out_ref.at[0], own)
    else:
        local = pltpu.make_async_copy(x_ref.at[me], out_ref.at[me], own)
    local.start()
    local.wait()
    for copy in copies:
        copy.wait()


def exchange(x, axis, sizes, collective_id, spread=False):
    count = sizes["loss"] * sizes["vars"] if axis == "group" else sizes[axis]
    shape = (count,) + x.shape if spread else x.shape
    return pl.pallas_call(
        functools.partial(exchange_kernel, axis, count, sizes, spread),
        out_shape=jax.ShapeDtypeStruct(shape, x.dtype),
        in_specs=[VMEM],
        out_specs=VMEM,
        scratch_shapes=[
            pltpu.SemaphoreType.DMA((count - 1,)),
            pltpu.SemaphoreType.DMA((count - 1,)),
            pltpu.SemaphoreType.DMA,
        ],
        compiler_params=pltpu.CompilerParams(
            collective_id=collective_id, has_side_effects=True
        ),
        name="exchange_%d" % collective_id,
    )(x)


def total_kernel(count, sizes, x_ref, out_ref, parts, acc, send, recv, send2, recv2, own):
    me = rank("proc", sizes)
    peers = [lax.rem(me + k, count) for k in range(1, count)]
    greet([place("proc", peer, sizes) for peer in peers])

    def copy(src, dst, sems, k, peer):
        made = pltpu.make_async_remote_copy(
            src_ref=src,
            dst_ref=dst,
            send_sem=sems[0].at[k],
            recv_sem=sems[1].at[k],
            device_id=place("proc", peer, sizes),
            device_id_type=MESH,
        )
        made.start()
        return made

    first = [copy(x_ref.at[peer], parts.at[k], (send, recv), k, peer) for k, peer in enumerate(peers)]
    for made in first:
        made.wait()
    value = x_ref[me]
    for k in range(count - 1):
        value = value + parts[k]
    acc[...] = value
    second = [copy(acc, out_ref.at[me], (send2, recv2), k, peer) for k, peer in enumerate(peers)]
    local = pltpu.make_async_copy(acc, out_ref.at[me], own)
    local.start()
    local.wait()
    for made in second:
        made.wait()


def proc_total(x, sizes, collective_id):
    count = sizes["proc"]
    sems = [pltpu.SemaphoreType.DMA((count - 1,)) for _ in range(4)]
    return pl.pallas_call(
        functools.partial(total_kernel, count, sizes),
        out_shape=jax.ShapeDtypeStruct(x.shape, x.dtype),
        in_specs=[VMEM],
        out_specs=VMEM,
        scratch_shapes=[
            pltpu.VMEM((count - 1,) + x.shape[1:], x.dtype),
            pltpu.VMEM(x.shape[1:], x.dtype),
        ]
        + sems
        + [pltpu.SemaphoreType.DMA],
        compiler_params=pltpu.CompilerParams(
            collective_id=collective_id, has_side_effects=True
        ),
        name="proc_total",
    )(x)


def harmonics_kernel(modes, var_count, spectra_ref, legendre_ref, harm_ref, power_ref):
    half = 2 * var_count
    sums = [jnp.zeros((half, LDEG), F32) for _ in range(3)]
    for m in range(modes):
        harm = jnp.dot(
            spectra_ref[m], legendre_ref[m], precision=HIGHEST, preferred_element_type=F32
        )
        harm_ref[m] = harm
        pred, true = harm[:half], harm[half:]
        sums = [sums[0] + pred * pred, sums[1] + true * true, sums[2] + pred * true]
    for i in range(3):
        power_ref[i] = sums[i][:var_count] + sums[i][var_count:]


def harmonics(spectra, legendre):
    modes, rows, _ = spectra.shape
    var_count = rows // 4
    return pl.pallas_call(
        functools.partial(harmonics_kernel, modes, var_count),
        out_shape=(
            jax.ShapeDtypeStruct((modes, rows, LDEG), F32),
            jax.ShapeDtypeStruct((3, var_count, LDEG), F32),
        ),
        in_specs=[VMEM, VMEM],
        out_specs=(VMEM, VMEM),
        name="harmonics",
    )(spectra, legendre)


def spectra_grad_kernel(modes, pack, procs, var_count, harm_ref, legendre_ref, gp_ref, gc_ref, out_ref):
    half = 2 * var_count
    gp = jnp.concatenate([gp_ref[...], gp_ref[...]], axis=0) * 2.0
    gc = jnp.concatenate([gc_ref[...], gc_ref[...]], axis=0)
    for hi in range(modes // pack):
        columns = []
        for lo in range(pack):
            m = hi * pack + lo
            harm = harm_ref[m]
            grad = gp * harm[:half] + gc * harm[half:]
            columns.append(
                lax.dot_general(
                    legendre_ref[m], grad, NT, precision=HIGHEST, preferred_element_type=F32
                )
            )
        block = jnp.concatenate(columns, axis=1)
        out_ref[:, hi] = block.reshape(procs, block.shape[0] // procs, block.shape[1])


def spectra_grad(harm, legendre, gp, gc, procs):
    modes, rows, _ = harm.shape
    lats = legendre.shape[1]
    var_count = rows // 4
    pack = min(modes, max(1, 128 // (2 * var_count)))
    return pl.pallas_call(
        functools.partial(spectra_grad_kernel, modes, pack, procs, var_count),
        out_shape=jax.ShapeDtypeStruct(
            (procs, modes // pack, lats // procs, pack * 2 * var_count), F32
        ),
        in_specs=[VMEM] * 4,
        out_specs=VMEM,
        name="spectra_grad",
    )(harm, legendre, gp, gc), pack


def attention_kernel(
    heads,
    cols,
    blocks,
    sizes,
    f_ref,
    coeff_ref,
    mix_ref,
    proj_ref,
    tok_ref,
    gain_ref,
    w_ref,
    out_ref,
    part,
    kept,
    got,
    mid,
    far,
    s1,
    r1,
    s2,
    r2,
):
    loss_count, var_count = sizes["loss"], sizes["vars"]
    loss, var = lax.axis_index("loss"), lax.axis_index("vars")
    near = [lax.rem(var + k, var_count) for k in range(1, var_count)]
    away = [lax.rem(loss + k, loss_count) for k in range(1, loss_count)]
    step = pl.program_id(0)
    rows = WR * cols

    @pl.when(step == 0)
    def _():
        greet(
            [place("vars", peer, sizes) for peer in near]
            + [place("loss", peer, sizes) for peer in away]
        )

    def near_copies(b):
        return [
            pltpu.make_async_remote_copy(
                src_ref=part.at[b, peer],
                dst_ref=got.at[b, k],
                send_sem=s1.at[b, k],
                recv_sem=r1.at[b, k],
                device_id=place("vars", peer, sizes),
                device_id_type=MESH,
            )
            for k, peer in enumerate(near)
        ]

    def away_copies(b):
        return [
            pltpu.make_async_remote_copy(
                src_ref=mid.at[b, peer],
                dst_ref=far.at[b, k],
                send_sem=s2.at[b, k],
                recv_sem=r2.at[b, k],
                device_id=place("loss", peer, sizes),
                device_id_type=MESH,
            )
            for k, peer in enumerate(away)
        ]

    def pass_on(b):
        for made in near_copies(b):
            made.wait()
        for j in range(loss_count):
            value = part[b, var, j].astype(F32)
            for k in range(var_count - 1):
                value = value + got[b, k, j].astype(F32)
            mid[b, j] = value.astype(BF16)
        for made in away_copies(b):
            made.start()

    pieces = []
    for o in range(4):
        y = jnp.dot(f_ref[o], coeff_ref[0], preferred_element_type=F32)
        half = y.shape[1] // WR
        pieces.append(
            jnp.concatenate([y[:, r * half : (r + 1) * half] for r in range(WR)], axis=0).astype(BF16)
        )
    tiles = jnp.concatenate(pieces, axis=1)
    mixed = jnp.dot(tiles, mix_ref[...], preferred_element_type=F32)
    width = heads * HEAD
    grad_out = mixed[:, :width].astype(BF16)
    kept[step] = mixed[:, width:]

    window_i = lax.rem(lax.broadcasted_iota(jnp.int32, (rows, rows), 0), cols) // WC
    window_j = lax.rem(lax.broadcasted_iota(jnp.int32, (rows, rows), 1), cols) // WC
    same = window_i == window_j
    scale = HEAD ** (-0.5)
    grads = [[], [], []]
    for h in range(heads):
        q, k, v = (
            proj_ref[0, :, (i * heads + h) * HEAD : (i * heads + h + 1) * HEAD] for i in range(3)
        )
        go = grad_out[:, h * HEAD : (h + 1) * HEAD]
        scores = lax.dot_general(q, k, NT, preferred_element_type=F32) * scale
        weights = jnp.where(same, jnp.exp(scores), 0.0)
        weights = weights / jnp.sum(weights, axis=-1, keepdims=True)
        rounded = weights.astype(BF16)
        first = (((0,), (0,)), ((), ()))
        grads[2].append(
            lax.dot_general(rounded, go, first, preferred_element_type=F32).astype(BF16)
        )
        grad_weights = lax.dot_general(go, v, NT, preferred_element_type=F32)
        inner = jnp.sum(weights * grad_weights, axis=-1, keepdims=True)
        score_round = (weights * (grad_weights - inner) * scale).astype(BF16)
        grads[0].append(jnp.dot(score_round, k, preferred_element_type=F32).astype(BF16))
        grads[1].append(
            lax.dot_general(score_round, q, first, preferred_element_type=F32).astype(BF16)
        )
    stacked = jnp.concatenate(grads[0] + grads[1] + grads[2], axis=1)
    grad_normed = lax.dot_general(stacked, w_ref[...], NT, preferred_element_type=F32)

    values = tok_ref[0].astype(F32)
    centred = values - jnp.mean(values, axis=-1, keepdims=True)
    inv_std = lax.rsqrt(jnp.mean(centred * centred, axis=-1, keepdims=True) + NORM_EPSILON)
    normed = centred * inv_std
    scaled = grad_normed * gain_ref[...]
    local = inv_std * (
        scaled
        - jnp.mean(scaled, axis=-1, keepdims=True)
        - normed * jnp.mean(scaled * normed, axis=-1, keepdims=True)
    )
    local = local.astype(BF16)
    share = local.shape[1] // (loss_count * var_count)
    for l in range(loss_count):
        for v in range(var_count):
            at = (l * var_count + v) * share
            part[step, v, l] = local[:, at : at + share]
    for made in near_copies(step):
        made.start()

    @pl.when(step > 0)
    def _():
        pass_on(step - 1)

    @pl.when(step == blocks - 1)
    def _():
        pass_on(blocks - 1)
        for b in range(blocks):
            for made in away_copies(b):
                made.wait()
            value = kept[b] + mid[b, loss].astype(F32)
            for k in range(loss_count - 1):
                value = value + far[b, k].astype(F32)
            out_ref[b] = value.astype(BF16)


def attention_backward(f_rolled, coeff, mix, projected, tokens, gain, w_flat, sizes, collective_id):
    blocks, rows, model = tokens.shape
    pairs = coeff.shape[0]
    cols = rows // WR
    per_pair = blocks // pairs
    depth = f_rolled.shape[2]
    width = projected.shape[2] // 3
    heads = width // HEAD
    loss_count, var_count = sizes["loss"], sizes["vars"]
    share = model // (loss_count * var_count)

    def whole(shape):
        return pl.BlockSpec(shape, lambda b: (0,) * len(shape))

    def per_block(shape):
        return pl.BlockSpec((1,) + shape, lambda b: (b,) + (0,) * len(shape))

    return pl.pallas_call(
        functools.partial(attention_kernel, heads, cols, blocks, sizes),
        grid=(blocks,),
        in_specs=[
            pl.BlockSpec((4, cols, depth), lambda b: (0, lax.rem(b, per_pair), 0)),
            pl.BlockSpec((1,) + coeff.shape[1:], lambda b: (b // per_pair, 0, 0)),
            whole(mix.shape),
            per_block((rows, 3 * width)),
            per_block((rows, model)),
            whole(gain.shape),
            whole(w_flat.shape),
        ],
        out_specs=whole((blocks, rows, share)),
        out_shape=jax.ShapeDtypeStruct((blocks, rows, share), BF16),
        scratch_shapes=[
            pltpu.VMEM((blocks, var_count, loss_count, rows, share), BF16),
            pltpu.VMEM((blocks, rows, share), F32),
            pltpu.VMEM((blocks, var_count - 1, loss_count, rows, share), BF16),
            pltpu.VMEM((blocks, loss_count, rows, share), BF16),
            pltpu.VMEM((blocks, loss_count - 1, rows, share), BF16),
            pltpu.SemaphoreType.DMA((blocks, var_count - 1)),
            pltpu.SemaphoreType.DMA((blocks, var_count - 1)),
            pltpu.SemaphoreType.DMA((blocks, loss_count - 1)),
            pltpu.SemaphoreType.DMA((blocks, loss_count - 1)),
        ],
        compiler_params=pltpu.CompilerParams(
            collective_id=collective_id, has_side_effects=True
        ),
        name="attention_backward",
    )(f_rolled, coeff, mix, projected, tokens, gain, w_flat)


def body(tokens, shift, w_qkv, w_proj, ln_gain, w_dec, prediction, target, legendre):
    sizes = {name: lax.axis_size(name) for name in ("proc", "loss", "vars")}
    procs = sizes["proc"]
    groups = (sizes["loss"], sizes["vars"])
    group_count = groups[0] * groups[1]
    modes = legendre.shape[0]
    lat_all = legendre.shape[1]
    modes_all = modes * procs
    var_count, lats = prediction.shape[0], prediction.shape[1]
    basis = fourier_basis(modes_all)
    row_count, col_count, model = tokens.shape
    offset = shift[0]
    head_local = w_qkv.shape[2]
    width = head_local * HEAD
    share = model // group_count

    to_modes = jnp.asarray(
        basis.reshape(2, LON, procs, modes).transpose(2, 0, 3, 1).reshape(-1, LON), F32
    )
    fields = jnp.concatenate([prediction.astype(F32), target]).reshape(-1, LON)
    spectra = lax.dot_general(to_modes, fields, NT, precision=HIGHEST)
    at_owner = exchange(spectra.reshape(procs, 2 * modes, -1), "proc", sizes, 1)
    at_owner = at_owner.reshape(procs, 2, modes, 2, var_count, lats).transpose(2, 3, 1, 4, 0, 5)
    harm, power = harmonics(at_owner.reshape(modes, 4 * var_count, lat_all), legendre)
    if power.size % (procs * 128) == 0:
        shaped = power.reshape(procs, -1, 128)
        power = proc_total(shaped, sizes, 2).reshape(power.shape)
    else:
        power = lax.psum(power, "proc")
    degree_terms, pullback = jax.vjp(amse_terms, power[0], power[1], power[2])
    amse = jnp.sum(degree_terms, axis=-1) / (LDEG * modes_all)
    weight_grad = lat_all * LON / (VARS * LDEG * modes_all)
    grad_pred, _, grad_cross = pullback(jnp.full(degree_terms.shape, weight_grad, F32))
    grad_spectra, pack = spectra_grad(harm, legendre, grad_pred, grad_cross, procs)
    banded = exchange(grad_spectra, "proc", sizes, 3)
    banded = banded.reshape(procs, modes // pack, lats, pack, 2, var_count)
    banded = banded.transpose(0, 1, 3, 4, 5, 2).reshape(2 * modes_all, var_count, lats)

    pairs = row_count // WR
    sent = banded.astype(BF16).reshape(2 * modes_all, var_count, pairs, WR, 4)
    sent = sent.transpose(0, 2, 3, 1, 4).reshape(2 * modes_all, -1)
    coeff = exchange(sent, "group", sizes, 4, spread=True)
    coeff = coeff.reshape(group_count, 2 * modes_all, pairs, WR, 4 * var_count)
    coeff = coeff.transpose(2, 1, 3, 0, 4).reshape(pairs, 2 * modes_all, -1)

    by_mode = basis.transpose(1, 2, 0).reshape(LON, 2 * modes_all)
    field_grad = lax.dot_general(
        banded.reshape(2 * modes_all, -1),
        jnp.asarray(by_mode, F32),
        (((0,), (1,)), ((), ())),
        precision=HIGHEST,
    ).reshape(var_count, lats, LON)

    decoder = w_dec.transpose(2, 0, 1, 3).reshape(4 * var_count * 4, model)
    through = lax.dot_general(
        decoder, w_proj.reshape(-1, model), NT, preferred_element_type=F32
    ).astype(BF16)
    mix = jnp.concatenate(
        [
            through.reshape(-1, group_count, width),
            decoder.reshape(-1, group_count, share),
        ],
        axis=2,
    ).transpose(1, 0, 2)
    me = rank("group", sizes)
    received = [lax.dynamic_index_in_dim(mix, me, 0, keepdims=False)]
    for k in range(1, group_count):
        block = lax.dynamic_index_in_dim(mix, lax.rem(me + k, group_count), 0, keepdims=False)
        ring = [(g, (g + k) % group_count) for g in range(group_count)]
        received.append(lax.ppermute(block, ("loss", "vars"), ring))
    mix = jnp.stack(received)
    mix = mix.reshape(group_count, 4, 4 * var_count, width + share).transpose(1, 0, 2, 3)
    mix = mix.reshape(-1, width + share)

    cols = 72
    split = (pairs, WR, col_count // cols, cols)
    rolled = jnp.roll(tokens, -offset, axis=1)
    rolled = rolled.reshape(split + (model,)).transpose(0, 2, 1, 3, 4)
    rolled = rolled.reshape(-1, WR * cols, model)
    values = rolled.astype(F32)
    centred = values - jnp.mean(values, axis=-1, keepdims=True)
    inv_std = lax.rsqrt(jnp.mean(centred * centred, axis=-1, keepdims=True) + NORM_EPSILON)
    norm_out = (centred * inv_std * ln_gain).astype(BF16)
    w_flat = w_qkv.reshape(model, 3 * width)
    projected = jnp.einsum(
        "brd,dk->brk", norm_out, w_flat, preferred_element_type=F32
    ).astype(BF16)
    by_column = jnp.asarray(
        by_mode.reshape(col_count, 4, 2 * modes_all).transpose(1, 0, 2), BF16
    )
    f_rolled = jnp.roll(by_column, -offset, axis=1)
    summed = attention_backward(
        f_rolled, coeff, mix, projected, rolled, ln_gain.reshape(1, model), w_flat, sizes, 6
    )
    summed = summed.reshape(pairs, col_count // cols, WR, cols, share).transpose(0, 2, 1, 3, 4)
    input_grad = jnp.roll(summed.reshape(row_count, col_count, share), offset, axis=1)
    return (amse, field_grad, input_grad)


def solution(mesh):
    return jax.shard_map(
        body,
        mesh=mesh,
        in_specs=(
            P("proc", None, None),
            P(),
            P(None, None, ("loss", "vars"), None),
            P(),
            P(),
            P(("loss", "vars"), None, None, None),
            P(("loss", "vars"), "proc", None),
            P(("loss", "vars"), "proc", None),
            P("proc", None, None),
        ),
        out_specs=(
            P(("loss", "vars")),
            P(("loss", "vars"), "proc", None),
            P("proc", None, ("loss", "vars")),
        ),
        check_vma=False,
    )
```

```python
import functools
import math

import jax
import jax.numpy as jnp
import numpy as np
from jax import lax
from jax.experimental import pallas as pl
from jax.experimental.pallas import tpu as pltpu
from jax.sharding import PartitionSpec as P

HEAD = 96
VARS = 64
LON = 1440
LDEG = 384
WR = 2
WC = 12

EPSILON = 1e-06
NORM_EPSILON = 1e-05
HIGHEST = lax.Precision.HIGHEST
MESH = pl.DeviceIdType.MESH
F32 = jnp.float32
BF16 = jnp.bfloat16
VMEM = pl.BlockSpec(memory_space=pltpu.VMEM)
NT = (((1,), (1,)), ((), ()))


def fourier_basis(mode_count):
    column = np.arange(LON, dtype=np.int64)
    wavenumber = np.arange(mode_count, dtype=np.int64)
    phase = (column[:, None] * wavenumber[None, :] % LON) * (2.0 * math.pi / LON)
    return np.stack([np.cos(phase), -np.sin(phase)]) / math.sqrt(LON)


def amse_terms(power_pred, power_true, crossed):
    amp_pred = jnp.sqrt(power_pred + EPSILON)
    amp_true = jnp.sqrt(power_true + EPSILON)
    return (amp_pred - amp_true) ** 2 + 2.0 * jnp.maximum(power_pred, power_true) * (
        1.0 - crossed / (amp_pred * amp_true)
    )


def place(axis, index, sizes):
    proc, loss, var = (lax.axis_index(name) for name in ("proc", "loss", "vars"))
    if axis == "proc":
        return (index, loss, var)
    if axis == "loss":
        return (proc, index, var)
    if axis == "vars":
        return (proc, loss, index)
    return (proc, index // sizes["vars"], lax.rem(index, sizes["vars"]))


def rank(axis, sizes):
    if axis == "group":
        return lax.axis_index("loss") * sizes["vars"] + lax.axis_index("vars")
    return lax.axis_index(axis)


def greet(pairs):
    barrier = pltpu.get_barrier_semaphore()
    for device in pairs:
        pl.semaphore_signal(barrier, inc=1, device_id=device, device_id_type=MESH)
    pl.semaphore_wait(barrier, len(pairs))


def exchange_kernel(axis, count, sizes, spread, x_ref, out_ref, send, recv, own):
    me = rank(axis, sizes)
    peers = [lax.rem(me + k, count) for k in range(1, count)]
    greet([place(axis, peer, sizes) for peer in peers])
    copies = []
    for k, peer in enumerate(peers):
        copies.append(
            pltpu.make_async_remote_copy(
                src_ref=x_ref if spread else x_ref.at[peer],
                dst_ref=out_ref.at[k + 1] if spread else out_ref.at[me],
                send_sem=send.at[k],
                recv_sem=recv.at[k],
                device_id=place(axis, peer, sizes),
                device_id_type=MESH,
            )
        )
        copies[-1].start()
    if spread:
        local = pltpu.make_async_copy(x_ref, out_ref.at[0], own)
    else:
        local = pltpu.make_async_copy(x_ref.at[me], out_ref.at[me], own)
    local.start()
    local.wait()
    for copy in copies:
        copy.wait()


def exchange(x, axis, sizes, collective_id, spread=False):
    count = sizes["loss"] * sizes["vars"] if axis == "group" else sizes[axis]
    shape = (count,) + x.shape if spread else x.shape
    return pl.pallas_call(
        functools.partial(exchange_kernel, axis, count, sizes, spread),
        out_shape=jax.ShapeDtypeStruct(shape, x.dtype),
        in_specs=[VMEM],
        out_specs=VMEM,
        scratch_shapes=[
            pltpu.SemaphoreType.DMA((count - 1,)),
            pltpu.SemaphoreType.DMA((count - 1,)),
            pltpu.SemaphoreType.DMA,
        ],
        compiler_params=pltpu.CompilerParams(
            collective_id=collective_id, has_side_effects=True
        ),
        name="exchange_%d" % collective_id,
    )(x)


def harmonics_kernel(modes, var_count, spectra_ref, legendre_ref, harm_ref, power_ref):
    half = 2 * var_count
    sums = [jnp.zeros((half, LDEG), F32) for _ in range(3)]
    for m in range(modes):
        harm = jnp.dot(
            spectra_ref[m], legendre_ref[m], precision=HIGHEST, preferred_element_type=F32
        )
        harm_ref[m] = harm
        pred, true = harm[:half], harm[half:]
        sums = [sums[0] + pred * pred, sums[1] + true * true, sums[2] + pred * true]
    for i in range(3):
        power_ref[i] = sums[i][:var_count] + sums[i][var_count:]


def harmonics(spectra, legendre):
    modes, rows, _ = spectra.shape
    var_count = rows // 4
    return pl.pallas_call(
        functools.partial(harmonics_kernel, modes, var_count),
        out_shape=(
            jax.ShapeDtypeStruct((modes, rows, LDEG), F32),
            jax.ShapeDtypeStruct((3, var_count, LDEG), F32),
        ),
        in_specs=[VMEM, VMEM],
        out_specs=(VMEM, VMEM),
        name="harmonics",
    )(spectra, legendre)


def spectra_grad_kernel(modes, pack, procs, var_count, harm_ref, legendre_ref, gp_ref, gc_ref, out_ref):
    half = 2 * var_count
    gp = jnp.concatenate([gp_ref[...], gp_ref[...]], axis=0) * 2.0
    gc = jnp.concatenate([gc_ref[...], gc_ref[...]], axis=0)
    for hi in range(modes // pack):
        columns = []
        for lo in range(pack):
            m = hi * pack + lo
            harm = harm_ref[m]
            grad = gp * harm[:half] + gc * harm[half:]
            columns.append(
                lax.dot_general(
                    legendre_ref[m], grad, NT, precision=HIGHEST, preferred_element_type=F32
                )
            )
        block = jnp.concatenate(columns, axis=1)
        out_ref[:, hi] = block.reshape(procs, block.shape[0] // procs, block.shape[1])


def spectra_grad(harm, legendre, gp, gc, procs):
    modes, rows, _ = harm.shape
    lats = legendre.shape[1]
    var_count = rows // 4
    pack = min(modes, max(1, 128 // (2 * var_count)))
    return pl.pallas_call(
        functools.partial(spectra_grad_kernel, modes, pack, procs, var_count),
        out_shape=jax.ShapeDtypeStruct(
            (procs, modes // pack, lats // procs, pack * 2 * var_count), F32
        ),
        in_specs=[VMEM] * 4,
        out_specs=VMEM,
        name="spectra_grad",
    )(harm, legendre, gp, gc)


def spectral_kernel(
    modes,
    pack,
    sizes,
    var_count,
    weight,
    spectra_ref,
    legendre_ref,
    terms_ref,
    banded_ref,
    coeff_ref,
    harm,
    power,
    parts,
    acc,
    outgoing,
    narrow,
    sa,
    ra,
    sb,
    rb,
    sc,
    rc,
    sd,
    rd,
):
    procs = sizes["proc"]
    group_count = sizes["loss"] * sizes["vars"]
    me, team = rank("proc", sizes), rank("group", sizes)
    peers = [lax.rem(me + k, procs) for k in range(1, procs)]
    mates = [lax.rem(team + k, group_count) for k in range(1, group_count)]
    greet(
        [place("proc", peer, sizes) for peer in peers]
        + [place("group", mate, sizes) for mate in mates]
    )
    half = 2 * var_count
    each = var_count // procs

    def copy(src, dst, send, recv, device):
        return pltpu.make_async_remote_copy(
            src_ref=src,
            dst_ref=dst,
            send_sem=send,
            recv_sem=recv,
            device_id=device,
            device_id_type=MESH,
        )

    sums = [jnp.zeros((half, LDEG), F32) for _ in range(3)]
    for m in range(modes):
        value = jnp.dot(
            spectra_ref[m], legendre_ref[m], precision=HIGHEST, preferred_element_type=F32
        )
        harm[m] = value
        pred, true = value[:half], value[half:]
        sums = [sums[0] + pred * pred, sums[1] + true * true, sums[2] + pred * true]
    for i in range(3):
        total = sums[i][:var_count] + sums[i][var_count:]
        for p in range(procs):
            power[p, i * each : (i + 1) * each] = total[p * each : (p + 1) * each]

    sent = [
        copy(power.at[peer], parts.at[k], sa.at[k], ra.at[k], place("proc", peer, sizes))
        for k, peer in enumerate(peers)
    ]
    for made in sent:
        made.start()
    for made in sent:
        made.wait()
    total = power[me]
    for k in range(procs - 1):
        total = total + parts[k]
    powers = [total[i * each : (i + 1) * each] for i in range(3)]
    terms, pullback = jax.vjp(amse_terms, *powers)
    grad_pred, _, grad_cross = pullback(jnp.full((each, LDEG), weight, F32))
    acc[...] = jnp.concatenate([2.0 * grad_pred, grad_cross, terms], axis=0)
    terms_ref[me] = acc[...]
    sent = [
        copy(acc, terms_ref.at[me], sb.at[k], rb.at[k], place("proc", peer, sizes))
        for k, peer in enumerate(peers)
    ]
    for made in sent:
        made.start()
    for made in sent:
        made.wait()
    gp = jnp.concatenate([terms_ref[p, :each] for p in range(procs)] * 2, axis=0)
    gc = jnp.concatenate([terms_ref[p, each : 2 * each] for p in range(procs)] * 2, axis=0)

    for hi in range(modes // pack):
        columns = []
        for lo in range(pack):
            value = harm[hi * pack + lo]
            grad = gp * value[:half] + gc * value[half:]
            columns.append(
                lax.dot_general(
                    legendre_ref[hi * pack + lo],
                    grad,
                    NT,
                    precision=HIGHEST,
                    preferred_element_type=F32,
                )
            )
        block = jnp.concatenate(columns, axis=1)
        outgoing[:, hi] = block.reshape(procs, block.shape[0] // procs, block.shape[1])
    sent = [
        copy(outgoing.at[peer], banded_ref.at[me], sc.at[k], rc.at[k], place("proc", peer, sizes))
        for k, peer in enumerate(peers)
    ]
    for made in sent:
        made.start()
    banded_ref[me] = outgoing[me]

    passed = []
    for k in range(procs):
        source = lax.rem(me + procs - k, procs)
        if k > 0:
            sent[k - 1].wait_recv()
        value = banded_ref[source].astype(BF16)
        narrow[source] = value
        coeff_ref[0, source] = value
        for j, mate in enumerate(mates):
            passed.append(
                copy(
                    narrow.at[source],
                    coeff_ref.at[j + 1, source],
                    sd.at[k, j],
                    rd.at[k, j],
                    place("group", mate, sizes),
                )
            )
            passed[-1].start()
    for made in sent:
        made.wait_send()
    for made in passed:
        made.wait()


def spectral(spectra, legendre, sizes, weight, collective_id):
    procs = sizes["proc"]
    group_count = sizes["loss"] * sizes["vars"]
    modes, rows, lats = spectra.shape
    var_count = rows // 4
    each = var_count // procs
    pack = min(modes, max(1, 128 // (2 * var_count)))
    block = (procs, modes // pack, lats // procs, pack * 2 * var_count)
    dma = pltpu.SemaphoreType.DMA
    return pl.pallas_call(
        functools.partial(spectral_kernel, modes, pack, sizes, var_count, weight),
        out_shape=(
            jax.ShapeDtypeStruct((procs, 3 * each, LDEG), F32),
            jax.ShapeDtypeStruct(block, F32),
            jax.ShapeDtypeStruct((group_count,) + block, BF16),
        ),
        in_specs=[VMEM, VMEM],
        out_specs=(VMEM, VMEM, VMEM),
        scratch_shapes=[
            pltpu.VMEM((modes, rows, LDEG), F32),
            pltpu.VMEM((procs, 3 * each, LDEG), F32),
            pltpu.VMEM((procs - 1, 3 * each, LDEG), F32),
            pltpu.VMEM((3 * each, LDEG), F32),
            pltpu.VMEM(block, F32),
            pltpu.VMEM(block, BF16),
        ]
        + [dma((procs - 1,)) for _ in range(6)]
        + [dma((procs, group_count - 1)) for _ in range(2)],
        compiler_params=pltpu.CompilerParams(
            collective_id=collective_id, has_side_effects=True
        ),
        name="spectral",
    )(spectra, legendre)


def attention_kernel(
    heads,
    cols,
    blocks,
    sizes,
    f_ref,
    coeff_ref,
    mix_ref,
    proj_ref,
    tok_ref,
    gain_ref,
    w_ref,
    out_ref,
    part,
    kept,
    got,
    mid,
    far,
    s1,
    r1,
    s2,
    r2,
):
    loss_count, var_count = sizes["loss"], sizes["vars"]
    loss, var = lax.axis_index("loss"), lax.axis_index("vars")
    near = [lax.rem(var + k, var_count) for k in range(1, var_count)]
    away = [lax.rem(loss + k, loss_count) for k in range(1, loss_count)]
    step = pl.program_id(0)
    rows = WR * cols

    @pl.when(step == 0)
    def _():
        greet(
            [place("vars", peer, sizes) for peer in near]
            + [place("loss", peer, sizes) for peer in away]
        )

    def near_copies(b):
        return [
            pltpu.make_async_remote_copy(
                src_ref=part.at[b, peer],
                dst_ref=got.at[b, k],
                send_sem=s1.at[b, k],
                recv_sem=r1.at[b, k],
                device_id=place("vars", peer, sizes),
                device_id_type=MESH,
            )
            for k, peer in enumerate(near)
        ]

    def away_copies(b):
        return [
            pltpu.make_async_remote_copy(
                src_ref=mid.at[b, peer],
                dst_ref=far.at[b, k],
                send_sem=s2.at[b, k],
                recv_sem=r2.at[b, k],
                device_id=place("loss", peer, sizes),
                device_id_type=MESH,
            )
            for k, peer in enumerate(away)
        ]

    def pass_on(b):
        for made in near_copies(b):
            made.wait()
        for j in range(loss_count):
            value = part[b, var, j].astype(F32)
            for k in range(var_count - 1):
                value = value + got[b, k, j].astype(F32)
            mid[b, j] = value.astype(BF16)
        for made in away_copies(b):
            made.start()

    pieces = []
    for o in range(4):
        y = jnp.dot(f_ref[o], coeff_ref[0], preferred_element_type=F32)
        half = y.shape[1] // WR
        pieces.append(
            jnp.concatenate([y[:, r * half : (r + 1) * half] for r in range(WR)], axis=0).astype(BF16)
        )
    tiles = jnp.concatenate(pieces, axis=1)
    mixed = jnp.dot(tiles, mix_ref[...], preferred_element_type=F32)
    width = heads * HEAD
    grad_out = mixed[:, :width].astype(BF16)
    kept[step] = mixed[:, width:]

    window_i = lax.rem(lax.broadcasted_iota(jnp.int32, (rows, rows), 0), cols) // WC
    window_j = lax.rem(lax.broadcasted_iota(jnp.int32, (rows, rows), 1), cols) // WC
    same = window_i == window_j
    scale = HEAD ** (-0.5)
    grads = [[], [], []]
    for h in range(heads):
        q, k, v = (
            proj_ref[0, :, (i * heads + h) * HEAD : (i * heads + h + 1) * HEAD] for i in range(3)
        )
        go = grad_out[:, h * HEAD : (h + 1) * HEAD]
        scores = lax.dot_general(q, k, NT, preferred_element_type=F32) * scale
        weights = jnp.where(same, jnp.exp(scores), 0.0)
        weights = weights / jnp.sum(weights, axis=-1, keepdims=True)
        rounded = weights.astype(BF16)
        first = (((0,), (0,)), ((), ()))
        grads[2].append(
            lax.dot_general(rounded, go, first, preferred_element_type=F32).astype(BF16)
        )
        grad_weights = lax.dot_general(go, v, NT, preferred_element_type=F32)
        inner = jnp.sum(weights * grad_weights, axis=-1, keepdims=True)
        score_round = (weights * (grad_weights - inner) * scale).astype(BF16)
        grads[0].append(jnp.dot(score_round, k, preferred_element_type=F32).astype(BF16))
        grads[1].append(
            lax.dot_general(score_round, q, first, preferred_element_type=F32).astype(BF16)
        )
    stacked = jnp.concatenate(grads[0] + grads[1] + grads[2], axis=1)
    grad_normed = lax.dot_general(stacked, w_ref[...], NT, preferred_element_type=F32)

    values = tok_ref[0].astype(F32)
    centred = values - jnp.mean(values, axis=-1, keepdims=True)
    inv_std = lax.rsqrt(jnp.mean(centred * centred, axis=-1, keepdims=True) + NORM_EPSILON)
    normed = centred * inv_std
    scaled = grad_normed * gain_ref[...]
    local = inv_std * (
        scaled
        - jnp.mean(scaled, axis=-1, keepdims=True)
        - normed * jnp.mean(scaled * normed, axis=-1, keepdims=True)
    )
    local = local.astype(BF16)
    share = local.shape[1] // (loss_count * var_count)
    for l in range(loss_count):
        for v in range(var_count):
            at = (l * var_count + v) * share
            part[step, v, l] = local[:, at : at + share]
    for made in near_copies(step):
        made.start()

    @pl.when(step > 0)
    def _():
        pass_on(step - 1)

    @pl.when(step == blocks - 1)
    def _():
        pass_on(blocks - 1)
        for b in range(blocks):
            for made in away_copies(b):
                made.wait()
            value = kept[b] + mid[b, loss].astype(F32)
            for k in range(loss_count - 1):
                value = value + far[b, k].astype(F32)
            out_ref[b] = value.astype(BF16)


def attention_backward(f_rolled, coeff, mix, projected, tokens, gain, w_flat, sizes, collective_id):
    blocks, rows, model = tokens.shape
    pairs = coeff.shape[0]
    cols = rows // WR
    per_pair = blocks // pairs
    depth = f_rolled.shape[2]
    width = projected.shape[2] // 3
    heads = width // HEAD
    loss_count, var_count = sizes["loss"], sizes["vars"]
    share = model // (loss_count * var_count)

    def whole(shape):
        return pl.BlockSpec(shape, lambda b: (0,) * len(shape))

    def per_block(shape):
        return pl.BlockSpec((1,) + shape, lambda b: (b,) + (0,) * len(shape))

    return pl.pallas_call(
        functools.partial(attention_kernel, heads, cols, blocks, sizes),
        grid=(blocks,),
        in_specs=[
            pl.BlockSpec((4, cols, depth), lambda b: (0, lax.rem(b, per_pair), 0)),
            pl.BlockSpec((1,) + coeff.shape[1:], lambda b: (b // per_pair, 0, 0)),
            whole(mix.shape),
            per_block((rows, 3 * width)),
            per_block((rows, model)),
            whole(gain.shape),
            whole(w_flat.shape),
        ],
        out_specs=whole((blocks, rows, share)),
        out_shape=jax.ShapeDtypeStruct((blocks, rows, share), BF16),
        scratch_shapes=[
            pltpu.VMEM((blocks, var_count, loss_count, rows, share), BF16),
            pltpu.VMEM((blocks, rows, share), F32),
            pltpu.VMEM((blocks, var_count - 1, loss_count, rows, share), BF16),
            pltpu.VMEM((blocks, loss_count, rows, share), BF16),
            pltpu.VMEM((blocks, loss_count - 1, rows, share), BF16),
            pltpu.SemaphoreType.DMA((blocks, var_count - 1)),
            pltpu.SemaphoreType.DMA((blocks, var_count - 1)),
            pltpu.SemaphoreType.DMA((blocks, loss_count - 1)),
            pltpu.SemaphoreType.DMA((blocks, loss_count - 1)),
        ],
        compiler_params=pltpu.CompilerParams(
            collective_id=collective_id, has_side_effects=True
        ),
        name="attention_backward",
    )(f_rolled, coeff, mix, projected, tokens, gain, w_flat)


def body(tokens, shift, w_qkv, w_proj, ln_gain, w_dec, prediction, target, legendre):
    sizes = {name: lax.axis_size(name) for name in ("proc", "loss", "vars")}
    procs = sizes["proc"]
    groups = (sizes["loss"], sizes["vars"])
    group_count = groups[0] * groups[1]
    modes = legendre.shape[0]
    lat_all = legendre.shape[1]
    modes_all = modes * procs
    var_count, lats = prediction.shape[0], prediction.shape[1]
    basis = fourier_basis(modes_all)
    row_count, col_count, model = tokens.shape
    offset = shift[0]
    head_local = w_qkv.shape[2]
    width = head_local * HEAD
    share = model // group_count

    ordered = basis.reshape(2, LON, procs, modes).transpose(2, 0, 3, 1).reshape(-1, LON)
    to_modes = jnp.asarray(ordered, F32)
    fields = jnp.concatenate([prediction.astype(F32), target]).reshape(-1, LON)
    spectra = lax.dot_general(to_modes, fields, NT, precision=HIGHEST)
    at_owner = exchange(spectra.reshape(procs, 2 * modes, -1), "proc", sizes, 1)
    at_owner = at_owner.reshape(procs, 2, modes, 2, var_count, lats).transpose(2, 3, 1, 4, 0, 5)
    at_owner = at_owner.reshape(modes, 4 * var_count, lat_all)
    weight_grad = lat_all * LON / (VARS * LDEG * modes_all)
    if var_count % procs == 0:
        terms, banded, coeff = spectral(at_owner, legendre, sizes, weight_grad, 2)
        each = var_count // procs
        degree_terms = terms[:, 2 * each :].reshape(var_count, LDEG)
    else:
        harm, power = harmonics(at_owner, legendre)
        power = lax.psum(power, "proc")
        degree_terms, pullback = jax.vjp(amse_terms, power[0], power[1], power[2])
        grad_pred, _, grad_cross = pullback(jnp.full(degree_terms.shape, weight_grad, F32))
        grad_spectra = spectra_grad(harm, legendre, grad_pred, grad_cross, procs)
        banded = exchange(grad_spectra, "proc", sizes, 3)
        coeff = exchange(banded.astype(BF16), "group", sizes, 4, spread=True)
    amse = jnp.sum(degree_terms, axis=-1) / (LDEG * modes_all)
    high, pack = banded.shape[1], modes // banded.shape[1]
    banded = banded.reshape(procs, high, lats, pack, 2, var_count)
    banded = banded.transpose(0, 4, 1, 3, 5, 2).reshape(2 * modes_all, var_count, lats)

    pairs = row_count // WR
    coeff = coeff.reshape(group_count, procs, high, pairs, WR, 4, pack, 2, var_count)
    coeff = coeff.transpose(3, 1, 7, 2, 6, 4, 0, 8, 5).reshape(pairs, 2 * modes_all, -1)

    field_grad = lax.dot_general(
        banded.reshape(2 * modes_all, -1),
        to_modes,
        (((0,), (0,)), ((), ())),
        precision=HIGHEST,
    ).reshape(var_count, lats, LON)

    decoder = w_dec.transpose(2, 0, 1, 3).reshape(4 * var_count * 4, model)
    through = lax.dot_general(
        decoder, w_proj.reshape(-1, model), NT, preferred_element_type=F32
    ).astype(BF16)
    mix = jnp.concatenate(
        [
            through.reshape(-1, group_count, width),
            decoder.reshape(-1, group_count, share),
        ],
        axis=2,
    ).transpose(1, 0, 2)
    me = rank("group", sizes)
    received = [lax.dynamic_index_in_dim(mix, me, 0, keepdims=False)]
    for k in range(1, group_count):
        block = lax.dynamic_index_in_dim(mix, lax.rem(me + k, group_count), 0, keepdims=False)
        ring = [(g, (g + k) % group_count) for g in range(group_count)]
        received.append(lax.ppermute(block, ("loss", "vars"), ring))
    mix = jnp.stack(received)
    mix = mix.reshape(group_count, 4, 4 * var_count, width + share).transpose(1, 0, 2, 3)
    mix = mix.reshape(-1, width + share)

    cols = 72
    split = (pairs, WR, col_count // cols, cols)
    rolled = jnp.roll(tokens, -offset, axis=1)
    rolled = rolled.reshape(split + (model,)).transpose(0, 2, 1, 3, 4)
    rolled = rolled.reshape(-1, WR * cols, model)
    values = rolled.astype(F32)
    centred = values - jnp.mean(values, axis=-1, keepdims=True)
    inv_std = lax.rsqrt(jnp.mean(centred * centred, axis=-1, keepdims=True) + NORM_EPSILON)
    norm_out = (centred * inv_std * ln_gain).astype(BF16)
    w_flat = w_qkv.reshape(model, 3 * width)
    projected = jnp.einsum(
        "brd,dk->brk", norm_out, w_flat, preferred_element_type=F32
    ).astype(BF16)
    by_column = jnp.asarray(ordered.T.reshape(col_count, 4, -1).transpose(1, 0, 2), BF16)
    f_rolled = jnp.roll(by_column, -offset, axis=1)
    summed = attention_backward(
        f_rolled, coeff, mix, projected, rolled, ln_gain.reshape(1, model), w_flat, sizes, 6
    )
    summed = summed.reshape(pairs, col_count // cols, WR, cols, share).transpose(0, 2, 1, 3, 4)
    input_grad = jnp.roll(summed.reshape(row_count, col_count, share), offset, axis=1)
    return (amse, field_grad, input_grad)


def solution(mesh):
    return jax.shard_map(
        body,
        mesh=mesh,
        in_specs=(
            P("proc", None, None),
            P(),
            P(None, None, ("loss", "vars"), None),
            P(),
            P(),
            P(("loss", "vars"), None, None, None),
            P(("loss", "vars"), "proc", None),
            P(("loss", "vars"), "proc", None),
            P("proc", None, None),
        ),
        out_specs=(
            P(("loss", "vars")),
            P(("loss", "vars"), "proc", None),
            P("proc", None, ("loss", "vars")),
        ),
        check_vma=False,
    )
```

```python
import functools
import math

import jax
import jax.numpy as jnp
import numpy as np
from jax import lax
from jax.experimental import pallas as pl
from jax.experimental.pallas import tpu as pltpu
from jax.sharding import PartitionSpec as P

HEAD = 96
VARS = 64
LON = 1440
LDEG = 384
WR = 2
WC = 12

EPSILON = 1e-06
NORM_EPSILON = 1e-05
HIGHEST = lax.Precision.HIGHEST
MESH = pl.DeviceIdType.MESH
F32 = jnp.float32
BF16 = jnp.bfloat16
VMEM = pl.BlockSpec(memory_space=pltpu.VMEM)
NT = (((1,), (1,)), ((), ()))


def fourier_basis(mode_count):
    column = np.arange(LON, dtype=np.int64)
    wavenumber = np.arange(mode_count, dtype=np.int64)
    phase = (column[:, None] * wavenumber[None, :] % LON) * (2.0 * math.pi / LON)
    return np.stack([np.cos(phase), -np.sin(phase)]) / math.sqrt(LON)


def amse_terms(power_pred, power_true, crossed):
    amp_pred = jnp.sqrt(power_pred + EPSILON)
    amp_true = jnp.sqrt(power_true + EPSILON)
    return (amp_pred - amp_true) ** 2 + 2.0 * jnp.maximum(power_pred, power_true) * (
        1.0 - crossed / (amp_pred * amp_true)
    )


def place(axis, index, sizes):
    proc, loss, var = (lax.axis_index(name) for name in ("proc", "loss", "vars"))
    if axis == "proc":
        return (index, loss, var)
    if axis == "loss":
        return (proc, index, var)
    if axis == "vars":
        return (proc, loss, index)
    return (proc, index // sizes["vars"], lax.rem(index, sizes["vars"]))


def rank(axis, sizes):
    if axis == "group":
        return lax.axis_index("loss") * sizes["vars"] + lax.axis_index("vars")
    return lax.axis_index(axis)


def greet(pairs):
    barrier = pltpu.get_barrier_semaphore()
    for device in pairs:
        pl.semaphore_signal(barrier, inc=1, device_id=device, device_id_type=MESH)
    pl.semaphore_wait(barrier, len(pairs))


def exchange_kernel(axis, count, sizes, spread, x_ref, out_ref, send, recv, own):
    me = rank(axis, sizes)
    peers = [lax.rem(me + k, count) for k in range(1, count)]
    greet([place(axis, peer, sizes) for peer in peers])
    copies = []
    for k, peer in enumerate(peers):
        copies.append(
            pltpu.make_async_remote_copy(
                src_ref=x_ref if spread else x_ref.at[peer],
                dst_ref=out_ref.at[k + 1] if spread else out_ref.at[me],
                send_sem=send.at[k],
                recv_sem=recv.at[k],
                device_id=place(axis, peer, sizes),
                device_id_type=MESH,
            )
        )
        copies[-1].start()
    if spread:
        local = pltpu.make_async_copy(x_ref, out_ref.at[0], own)
    else:
        local = pltpu.make_async_copy(x_ref.at[me], out_ref.at[me], own)
    local.start()
    local.wait()
    for copy in copies:
        copy.wait()


def exchange(x, axis, sizes, collective_id, spread=False):
    count = sizes["loss"] * sizes["vars"] if axis == "group" else sizes[axis]
    shape = (count,) + x.shape if spread else x.shape
    return pl.pallas_call(
        functools.partial(exchange_kernel, axis, count, sizes, spread),
        out_shape=jax.ShapeDtypeStruct(shape, x.dtype),
        in_specs=[VMEM],
        out_specs=VMEM,
        scratch_shapes=[
            pltpu.SemaphoreType.DMA((count - 1,)),
            pltpu.SemaphoreType.DMA((count - 1,)),
            pltpu.SemaphoreType.DMA,
        ],
        compiler_params=pltpu.CompilerParams(
            collective_id=collective_id, has_side_effects=True
        ),
        name="exchange_%d" % collective_id,
    )(x)


def harmonics_kernel(modes, var_count, spectra_ref, legendre_ref, harm_ref, power_ref):
    half = 2 * var_count
    sums = [jnp.zeros((half, LDEG), F32) for _ in range(3)]
    for m in range(modes):
        harm = jnp.dot(
            spectra_ref[m], legendre_ref[m], precision=HIGHEST, preferred_element_type=F32
        )
        harm_ref[m] = harm
        pred, true = harm[:half], harm[half:]
        sums = [sums[0] + pred * pred, sums[1] + true * true, sums[2] + pred * true]
    for i in range(3):
        power_ref[i] = sums[i][:var_count] + sums[i][var_count:]


def harmonics(spectra, legendre):
    modes, rows, _ = spectra.shape
    var_count = rows // 4
    return pl.pallas_call(
        functools.partial(harmonics_kernel, modes, var_count),
        out_shape=(
            jax.ShapeDtypeStruct((modes, rows, LDEG), F32),
            jax.ShapeDtypeStruct((3, var_count, LDEG), F32),
        ),
        in_specs=[VMEM, VMEM],
        out_specs=(VMEM, VMEM),
        name="harmonics",
    )(spectra, legendre)


def spectral_kernel(
    modes,
    sizes,
    var_count,
    weight,
    spectra_ref,
    legendre_ref,
    terms_ref,
    banded_ref,
    coeff_ref,
    harm,
    power,
    parts,
    acc,
    rows,
    outgoing,
    narrow,
    sa,
    ra,
    sb,
    rb,
    sc,
    rc,
    sd,
    rd,
):
    procs = sizes["proc"]
    group_count = sizes["loss"] * sizes["vars"]
    me, team = rank("proc", sizes), rank("group", sizes)
    peers = [lax.rem(me + k, procs) for k in range(1, procs)]
    mates = [lax.rem(team + k, group_count) for k in range(1, group_count)]
    greet(
        [place("proc", peer, sizes) for peer in peers]
        + [place("group", mate, sizes) for mate in mates]
    )
    half = 2 * var_count
    each = var_count // procs

    def copy(src, dst, send, recv, device):
        return pltpu.make_async_remote_copy(
            src_ref=src,
            dst_ref=dst,
            send_sem=send,
            recv_sem=recv,
            device_id=device,
            device_id_type=MESH,
        )

    sums = [jnp.zeros((half, LDEG), F32) for _ in range(3)]
    for m in range(modes):
        value = jnp.dot(
            spectra_ref[m], legendre_ref[m], precision=HIGHEST, preferred_element_type=F32
        )
        harm[m] = value
        pred, true = value[:half], value[half:]
        sums = [sums[0] + pred * pred, sums[1] + true * true, sums[2] + pred * true]
    for i in range(3):
        total = sums[i][:var_count] + sums[i][var_count:]
        for p in range(procs):
            power[p, i * each : (i + 1) * each] = total[p * each : (p + 1) * each]

    sent = [
        copy(power.at[peer], parts.at[k], sa.at[k], ra.at[k], place("proc", peer, sizes))
        for k, peer in enumerate(peers)
    ]
    for made in sent:
        made.start()
    for made in sent:
        made.wait()
    total = power[me]
    for k in range(procs - 1):
        total = total + parts[k]
    powers = [total[i * each : (i + 1) * each] for i in range(3)]
    terms, pullback = jax.vjp(amse_terms, *powers)
    grad_pred, _, grad_cross = pullback(jnp.full((each, LDEG), weight, F32))
    acc[...] = jnp.concatenate([2.0 * grad_pred, grad_cross, terms], axis=0)
    terms_ref[me] = acc[...]
    sent = [
        copy(acc, terms_ref.at[me], sb.at[k], rb.at[k], place("proc", peer, sizes))
        for k, peer in enumerate(peers)
    ]
    for made in sent:
        made.start()
    for made in sent:
        made.wait()
    gp = jnp.concatenate([terms_ref[p, :each] for p in range(procs)] * 2, axis=0)
    gc = jnp.concatenate([terms_ref[p, each : 2 * each] for p in range(procs)] * 2, axis=0)

    lats = legendre_ref.shape[1]
    own = lats // procs
    for m in range(modes):
        value = harm[m]
        grad = gp * value[:half] + gc * value[half:]
        rows[m * half : (m + 1) * half, :lats] = lax.dot_general(
            grad, legendre_ref[m], NT, precision=HIGHEST, preferred_element_type=F32
        )
    by_var = [rows[pl.ds(v, 2 * modes, stride=var_count), :] for v in range(var_count)]
    for q in range(procs):
        outgoing[q] = jnp.concatenate(
            [
                by_var[v][:, q * own + 4 * r : q * own + 4 * r + 4]
                for r in range(own // 4)
                for v in range(var_count)
            ],
            axis=1,
        )
    sent = [
        copy(outgoing.at[peer], banded_ref.at[me], sc.at[k], rc.at[k], place("proc", peer, sizes))
        for k, peer in enumerate(peers)
    ]
    for made in sent:
        made.start()
    banded_ref[me] = outgoing[me]

    passed = []
    for k in range(procs):
        source = lax.rem(me + procs - k, procs)
        if k > 0:
            sent[k - 1].wait_recv()
        value = banded_ref[source].astype(BF16)
        narrow[source] = value
        coeff_ref[0, source] = value
        for j, mate in enumerate(mates):
            passed.append(
                copy(
                    narrow.at[source],
                    coeff_ref.at[j + 1, source],
                    sd.at[k, j],
                    rd.at[k, j],
                    place("group", mate, sizes),
                )
            )
            passed[-1].start()
    for made in sent:
        made.wait_send()
    for made in passed:
        made.wait()


def spectral(spectra, legendre, sizes, weight, collective_id):
    procs = sizes["proc"]
    group_count = sizes["loss"] * sizes["vars"]
    modes, rows, lats = spectra.shape
    var_count = rows // 4
    each = var_count // procs
    block = (procs, 2 * modes, var_count * lats // procs)
    dma = pltpu.SemaphoreType.DMA
    return pl.pallas_call(
        functools.partial(spectral_kernel, modes, sizes, var_count, weight),
        out_shape=(
            jax.ShapeDtypeStruct((procs, 3 * each, LDEG), F32),
            jax.ShapeDtypeStruct(block, F32),
            jax.ShapeDtypeStruct((group_count,) + block, BF16),
        ),
        in_specs=[VMEM, VMEM],
        out_specs=(VMEM, VMEM, VMEM),
        scratch_shapes=[
            pltpu.VMEM((modes, rows, LDEG), F32),
            pltpu.VMEM((procs, 3 * each, LDEG), F32),
            pltpu.VMEM((procs - 1, 3 * each, LDEG), F32),
            pltpu.VMEM((3 * each, LDEG), F32),
            pltpu.VMEM((2 * modes * var_count, pl.cdiv(lats, 128) * 128), F32),
            pltpu.VMEM(block, F32),
            pltpu.VMEM(block, BF16),
        ]
        + [dma((procs - 1,)) for _ in range(6)]
        + [dma((procs, group_count - 1)) for _ in range(2)],
        compiler_params=pltpu.CompilerParams(
            collective_id=collective_id, has_side_effects=True
        ),
        name="spectral",
    )(spectra, legendre)


def attention_kernel(
    heads,
    cols,
    blocks,
    sizes,
    f_ref,
    coeff_ref,
    mix_ref,
    proj_ref,
    tok_ref,
    gain_ref,
    w_ref,
    out_ref,
    part,
    kept,
    got,
    mid,
    far,
    s1,
    r1,
    s2,
    r2,
):
    loss_count, var_count = sizes["loss"], sizes["vars"]
    loss, var = lax.axis_index("loss"), lax.axis_index("vars")
    near = [lax.rem(var + k, var_count) for k in range(1, var_count)]
    away = [lax.rem(loss + k, loss_count) for k in range(1, loss_count)]
    step = pl.program_id(0)
    rows = WR * cols

    @pl.when(step == 0)
    def _():
        greet(
            [place("vars", peer, sizes) for peer in near]
            + [place("loss", peer, sizes) for peer in away]
        )

    def near_copies(b):
        return [
            pltpu.make_async_remote_copy(
                src_ref=part.at[b, peer],
                dst_ref=got.at[b, k],
                send_sem=s1.at[b, k],
                recv_sem=r1.at[b, k],
                device_id=place("vars", peer, sizes),
                device_id_type=MESH,
            )
            for k, peer in enumerate(near)
        ]

    def away_copies(b):
        return [
            pltpu.make_async_remote_copy(
                src_ref=mid.at[b, peer],
                dst_ref=far.at[b, k],
                send_sem=s2.at[b, k],
                recv_sem=r2.at[b, k],
                device_id=place("loss", peer, sizes),
                device_id_type=MESH,
            )
            for k, peer in enumerate(away)
        ]

    def pass_on(b):
        for made in near_copies(b):
            made.wait()
        for j in range(loss_count):
            value = part[b, var, j].astype(F32)
            for k in range(var_count - 1):
                value = value + got[b, k, j].astype(F32)
            mid[b, j] = value.astype(BF16)
        for made in away_copies(b):
            made.start()

    pieces = []
    for o in range(4):
        y = jnp.dot(f_ref[o], coeff_ref[0], preferred_element_type=F32)
        half = y.shape[1] // WR
        pieces.append(
            jnp.concatenate([y[:, r * half : (r + 1) * half] for r in range(WR)], axis=0).astype(BF16)
        )
    tiles = jnp.concatenate(pieces, axis=1)
    mixed = jnp.dot(tiles, mix_ref[...], preferred_element_type=F32)
    width = heads * HEAD
    grad_out = mixed[:, :width].astype(BF16)
    kept[step] = mixed[:, width:]

    window_i = lax.rem(lax.broadcasted_iota(jnp.int32, (rows, rows), 0), cols) // WC
    window_j = lax.rem(lax.broadcasted_iota(jnp.int32, (rows, rows), 1), cols) // WC
    same = window_i == window_j
    scale = HEAD ** (-0.5)
    grads = [[], [], []]
    for h in range(heads):
        q, k, v = (
            proj_ref[0, :, (i * heads + h) * HEAD : (i * heads + h + 1) * HEAD] for i in range(3)
        )
        go = grad_out[:, h * HEAD : (h + 1) * HEAD]
        scores = lax.dot_general(q, k, NT, preferred_element_type=F32) * scale
        weights = jnp.where(same, jnp.exp(scores), 0.0)
        weights = weights / jnp.sum(weights, axis=-1, keepdims=True)
        rounded = weights.astype(BF16)
        first = (((0,), (0,)), ((), ()))
        grads[2].append(
            lax.dot_general(rounded, go, first, preferred_element_type=F32).astype(BF16)
        )
        grad_weights = lax.dot_general(go, v, NT, preferred_element_type=F32)
        inner = jnp.sum(weights * grad_weights, axis=-1, keepdims=True)
        score_round = (weights * (grad_weights - inner) * scale).astype(BF16)
        grads[0].append(jnp.dot(score_round, k, preferred_element_type=F32).astype(BF16))
        grads[1].append(
            lax.dot_general(score_round, q, first, preferred_element_type=F32).astype(BF16)
        )
    stacked = jnp.concatenate(grads[0] + grads[1] + grads[2], axis=1)
    grad_normed = lax.dot_general(stacked, w_ref[...], NT, preferred_element_type=F32)

    values = tok_ref[0].astype(F32)
    centred = values - jnp.mean(values, axis=-1, keepdims=True)
    inv_std = lax.rsqrt(jnp.mean(centred * centred, axis=-1, keepdims=True) + NORM_EPSILON)
    normed = centred * inv_std
    scaled = grad_normed * gain_ref[...]
    local = inv_std * (
        scaled
        - jnp.mean(scaled, axis=-1, keepdims=True)
        - normed * jnp.mean(scaled * normed, axis=-1, keepdims=True)
    )
    local = local.astype(BF16)
    share = local.shape[1] // (loss_count * var_count)
    for l in range(loss_count):
        for v in range(var_count):
            at = (l * var_count + v) * share
            part[step, v, l] = local[:, at : at + share]
    for made in near_copies(step):
        made.start()

    @pl.when(step > 0)
    def _():
        pass_on(step - 1)

    @pl.when(step == blocks - 1)
    def _():
        pass_on(blocks - 1)
        for b in range(blocks):
            for made in away_copies(b):
                made.wait()
            value = kept[b] + mid[b, loss].astype(F32)
            for k in range(loss_count - 1):
                value = value + far[b, k].astype(F32)
            out_ref[b] = value.astype(BF16)


def attention_backward(f_rolled, coeff, mix, projected, tokens, gain, w_flat, sizes, collective_id):
    blocks, rows, model = tokens.shape
    pairs = coeff.shape[0]
    cols = rows // WR
    per_pair = blocks // pairs
    depth = f_rolled.shape[2]
    width = projected.shape[2] // 3
    heads = width // HEAD
    loss_count, var_count = sizes["loss"], sizes["vars"]
    share = model // (loss_count * var_count)

    def whole(shape):
        return pl.BlockSpec(shape, lambda b: (0,) * len(shape))

    def per_block(shape):
        return pl.BlockSpec((1,) + shape, lambda b: (b,) + (0,) * len(shape))

    return pl.pallas_call(
        functools.partial(attention_kernel, heads, cols, blocks, sizes),
        grid=(blocks,),
        in_specs=[
            pl.BlockSpec((4, cols, depth), lambda b: (0, lax.rem(b, per_pair), 0)),
            pl.BlockSpec((1,) + coeff.shape[1:], lambda b: (b // per_pair, 0, 0)),
            whole(mix.shape),
            per_block((rows, 3 * width)),
            per_block((rows, model)),
            whole(gain.shape),
            whole(w_flat.shape),
        ],
        out_specs=whole((blocks, rows, share)),
        out_shape=jax.ShapeDtypeStruct((blocks, rows, share), BF16),
        scratch_shapes=[
            pltpu.VMEM((blocks, var_count, loss_count, rows, share), BF16),
            pltpu.VMEM((blocks, rows, share), F32),
            pltpu.VMEM((blocks, var_count - 1, loss_count, rows, share), BF16),
            pltpu.VMEM((blocks, loss_count, rows, share), BF16),
            pltpu.VMEM((blocks, loss_count - 1, rows, share), BF16),
            pltpu.SemaphoreType.DMA((blocks, var_count - 1)),
            pltpu.SemaphoreType.DMA((blocks, var_count - 1)),
            pltpu.SemaphoreType.DMA((blocks, loss_count - 1)),
            pltpu.SemaphoreType.DMA((blocks, loss_count - 1)),
        ],
        compiler_params=pltpu.CompilerParams(
            collective_id=collective_id, has_side_effects=True
        ),
        name="attention_backward",
    )(f_rolled, coeff, mix, projected, tokens, gain, w_flat)


def body(tokens, shift, w_qkv, w_proj, ln_gain, w_dec, prediction, target, legendre):
    sizes = {name: lax.axis_size(name) for name in ("proc", "loss", "vars")}
    procs = sizes["proc"]
    groups = (sizes["loss"], sizes["vars"])
    group_count = groups[0] * groups[1]
    modes = legendre.shape[0]
    lat_all = legendre.shape[1]
    modes_all = modes * procs
    var_count, lats = prediction.shape[0], prediction.shape[1]
    basis = fourier_basis(modes_all)
    row_count, col_count, model = tokens.shape
    offset = shift[0]
    head_local = w_qkv.shape[2]
    width = head_local * HEAD
    share = model // group_count

    ordered = basis.transpose(2, 0, 1).reshape(-1, LON)
    to_modes = jnp.asarray(ordered, F32)
    fields = jnp.concatenate([prediction.astype(F32), target]).reshape(-1, LON)
    spectra = lax.dot_general(to_modes, fields, NT, precision=HIGHEST)
    at_owner = exchange(spectra.reshape(procs, 2 * modes, -1), "proc", sizes, 1)
    at_owner = at_owner.reshape(procs, modes, 2, 2, var_count, lats).transpose(1, 3, 2, 4, 0, 5)
    at_owner = at_owner.reshape(modes, 4 * var_count, lat_all)
    weight_grad = lat_all * LON / (VARS * LDEG * modes_all)
    if var_count % procs == 0:
        terms, banded, coeff = spectral(at_owner, legendre, sizes, weight_grad, 2)
        each = var_count // procs
        degree_terms = terms[:, 2 * each :].reshape(var_count, LDEG)
    else:
        harm, power = harmonics(at_owner, legendre)
        power = lax.psum(power, "proc")
        degree_terms, pullback = jax.vjp(amse_terms, power[0], power[1], power[2])
        grad_pred, _, grad_cross = pullback(jnp.full(degree_terms.shape, weight_grad, F32))
        harm = harm.reshape(modes, 2, 2, var_count, LDEG)
        grad_harm = 2.0 * grad_pred * harm[:, 0] + grad_cross * harm[:, 1]
        grad_spectra = jnp.einsum("mcvl,mal->mcva", grad_harm, legendre, precision=HIGHEST)
        grad_spectra = grad_spectra.reshape(modes, 2, var_count, procs, lats // 4, 4)
        grad_spectra = grad_spectra.transpose(3, 0, 1, 4, 2, 5).reshape(procs, 2 * modes, -1)
        banded = exchange(grad_spectra, "proc", sizes, 3)
        coeff = exchange(banded.astype(BF16), "group", sizes, 4, spread=True)
    amse = jnp.sum(degree_terms, axis=-1) / (LDEG * modes_all)
    pairs = row_count // WR
    banded = banded.reshape(2 * modes_all, row_count, var_count, 4).transpose(0, 2, 1, 3)
    coeff = coeff.reshape(group_count, 2 * modes_all, pairs, WR, 4 * var_count)
    coeff = coeff.transpose(2, 1, 3, 0, 4).reshape(pairs, 2 * modes_all, -1)

    field_grad = lax.dot_general(
        banded.reshape(2 * modes_all, -1),
        to_modes,
        (((0,), (0,)), ((), ())),
        precision=HIGHEST,
    ).reshape(var_count, lats, LON)

    decoder = w_dec.transpose(2, 0, 1, 3).reshape(4 * var_count * 4, model)
    through = lax.dot_general(
        decoder, w_proj.reshape(-1, model), NT, preferred_element_type=F32
    ).astype(BF16)
    mix = jnp.concatenate(
        [
            through.reshape(-1, group_count, width),
            decoder.reshape(-1, group_count, share),
        ],
        axis=2,
    ).transpose(1, 0, 2)
    me = rank("group", sizes)
    received = [lax.dynamic_index_in_dim(mix, me, 0, keepdims=False)]
    for k in range(1, group_count):
        block = lax.dynamic_index_in_dim(mix, lax.rem(me + k, group_count), 0, keepdims=False)
        ring = [(g, (g + k) % group_count) for g in range(group_count)]
        received.append(lax.ppermute(block, ("loss", "vars"), ring))
    mix = jnp.stack(received)
    mix = mix.reshape(group_count, 4, 4 * var_count, width + share).transpose(1, 0, 2, 3)
    mix = mix.reshape(-1, width + share)

    cols = 120
    split = (pairs, WR, col_count // cols, cols)
    rolled = jnp.roll(tokens, -offset, axis=1)
    rolled = rolled.reshape(split + (model,)).transpose(0, 2, 1, 3, 4)
    rolled = rolled.reshape(-1, WR * cols, model)
    values = rolled.astype(F32)
    centred = values - jnp.mean(values, axis=-1, keepdims=True)
    inv_std = lax.rsqrt(jnp.mean(centred * centred, axis=-1, keepdims=True) + NORM_EPSILON)
    norm_out = (centred * inv_std * ln_gain).astype(BF16)
    w_flat = w_qkv.reshape(model, 3 * width)
    projected = jnp.einsum(
        "brd,dk->brk", norm_out, w_flat, preferred_element_type=F32
    ).astype(BF16)
    by_column = jnp.asarray(ordered.T.reshape(col_count, 4, -1).transpose(1, 0, 2), BF16)
    f_rolled = jnp.roll(by_column, -offset, axis=1)
    summed = attention_backward(
        f_rolled, coeff, mix, projected, rolled, ln_gain.reshape(1, model), w_flat, sizes, 6
    )
    summed = summed.reshape(pairs, col_count // cols, WR, cols, share).transpose(0, 2, 1, 3, 4)
    input_grad = jnp.roll(summed.reshape(row_count, col_count, share), offset, axis=1)
    return (amse, field_grad, input_grad)


def solution(mesh):
    return jax.shard_map(
        body,
        mesh=mesh,
        in_specs=(
            P("proc", None, None),
            P(),
            P(None, None, ("loss", "vars"), None),
            P(),
            P(),
            P(("loss", "vars"), None, None, None),
            P(("loss", "vars"), "proc", None),
            P(("loss", "vars"), "proc", None),
            P("proc", None, None),
        ),
        out_specs=(
            P(("loss", "vars")),
            P(("loss", "vars"), "proc", None),
            P("proc", None, ("loss", "vars")),
        ),
        check_vma=False,
    )
```
